32 devices in a mesh: dp: 4 (over z), ctx: 4 (over y, x), tp: 2 (over core).
Axes of the slice: x: 2, y: 2, z: 4, core: 2. Of those that a mesh axis runs over, the one named last changes fastest.
Arguments:
- tokens: bfloat16 [5120, 2048], P(('dp', 'ctx')), may hold values from -6 to 6
- cotangent: bfloat16 [5120, 2048], P(('dp', 'ctx')), may hold values from -6 to 6
- lengths: int32 [4, 3], P('dp'), may hold values from 1 to 1024, 1280 in all within a row
- deal_order: int32 [4, 1280], P('dp'), may hold values from 0 to 1279, each once within a row
- routes: int32 [5120, 6], P(('dp', 'ctx')), may hold values from 0 to 15, all different within a row; in each aligned block of 320 rows (0 to 319, 320 to 639, ...) at most 160 rows name the same one
- attn_gain: bfloat16 [2048], P(('dp', 'ctx')), may hold values from 0.099609375 to 1.8984375
- q_weight: bfloat16 [2048, 3072], P(('dp', 'ctx'), 'tp'), may hold values from -0.125 to 0.125
- kv_down: bfloat16 [2048, 576], P(('dp', 'ctx')), may hold values from -0.125 to 0.125
- latent_gain: bfloat16 [512], P(('dp', 'ctx')), may hold values from 0.099609375 to 1.8984375
- kv_up: bfloat16 [512, 4096], P(('dp', 'ctx'), 'tp'), may hold values from -0.25 to 0.25
- out_weight: bfloat16 [2048, 2048], P('tp', ('dp', 'ctx')), may hold values from -0.75 to 0.75
- ffn_gain: bfloat16 [2048], P(('dp', 'ctx')), may hold values from 0.099609375 to 1.8984375
- router: bfloat16 [2048, 16], P(('dp', 'ctx')), may hold values from -0.0625 to 0.0625
- shared_gate: bfloat16 [2048, 2816], P(('dp', 'ctx'), 'tp'), may hold values from -0.125 to 0.125
- shared_up: bfloat16 [2048, 2816], P(('dp', 'ctx'), 'tp'), may hold values from -0.125 to 0.125
- shared_down: bfloat16 [2816, 2048], P('tp', ('dp', 'ctx')), may hold values from -0.109375 to 0.109375
- expert_gate: bfloat16 [16, 2048, 1408], P(('dp', 'ctx'), None, 'tp'), may hold values from -0.125 to 0.125
- expert_up: bfloat16 [16, 2048, 1408], P(('dp', 'ctx'), None, 'tp'), may hold values from -0.125 to 0.125
- expert_down: bfloat16 [16, 1408, 2048], P(('dp', 'ctx'), 'tp'), may hold values from -2.5 to 2.5
Outputs:
- output: bfloat16 [5120, 2048], P(('dp', 'ctx'))
- input_grad: float32 [5120, 2048], P(('dp', 'ctx'))
- attn_gain_grad: float32 [2048], P(('dp', 'ctx'))
- q_weight_grad: float32 [2048, 3072], P(('dp', 'ctx'), 'tp')
- kv_down_grad: float32 [2048, 576], P(('dp', 'ctx'))
- latent_gain_grad: float32 [512], P(('dp', 'ctx'))
- kv_up_grad: float32 [512, 4096], P(('dp', 'ctx'), 'tp')
- out_weight_grad: float32 [2048, 2048], P('tp', ('dp', 'ctx'))
- ffn_gain_grad: float32 [2048], P(('dp', 'ctx'))
- router_grad: float32 [2048, 16], P(('dp', 'ctx'))
- shared_gate_grad: float32 [2048, 2816], P(('dp', 'ctx'), 'tp')
- shared_up_grad: float32 [2048, 2816], P(('dp', 'ctx'), 'tp')
- shared_down_grad: float32 [2816, 2048], P('tp', ('dp', 'ctx'))
- expert_gate_grad: float32 [16, 2048, 1408], P(('dp', 'ctx'), None, 'tp')
- expert_up_grad: float32 [16, 2048, 1408], P(('dp', 'ctx'), None, 'tp')
- expert_down_grad: float32 [16, 1408, 2048], P(('dp', 'ctx'), 'tp')
The draws below stay inside these ranges and needn't reach their ends.
Inputs may be any that keep to these rules, and one draw needn't show every extreme that they name: Each row holds 3 lengths that sum to 1280; the longest is exactly 1024. `deal_order`: each row is a permutation of 0 to 1279. `routes`: each row names 6 different experts. In the 320 rows of one device no expert is named more than 160 times, a bound that some block reaches.
All inputs are finite; a program needn't handle non-finite values.
Results may differ from the reference program's by a relative error of at most 0.024.
Values may be sent and summed in bfloat16 or wider, within the bound.
No kernel may reach another device: no remote copies, remote signals or barrier semaphores. Data moves between devices by JAX's collectives and lax.ppermute only.
A program may use at most 320 MiB of HBM per device.

```python
import math
import jax
import jax.numpy as jnp
import numpy as np
from jax import lax

MODEL_WIDTH = 2048
H = 16
NOPE = 128
ROPE = 64
VDIM = 128
KV_RANK = 512
FF_EXP = 1408
TOP = 6
SEQS = 3
TOK_DEV = 320
FF_SH = 2816
EXPERTS = 16
GROUP = 1280
GROUPS = 4
MAXLEN = 1024
CAP = 160
TOKEN_TOTAL = 5120
N_DP = 4
N_CTX = 4
N_TP = 2


def steps_of(key, shape, shards, least, top_value):
    def one(axis_at, parts):
        draws = jax.random.uniform(jax.random.fold_in(jax.random.fold_in(key, 6), axis_at), (parts,), jnp.float32, least / len(shards), top_value / len(shards))
        return jnp.repeat(jnp.exp(draws), shape[axis_at] // parts).reshape((-1,) + (1,) * (len(shape) - axis_at - 1))

    factor_of = one(*shards[0])
    for cut in shards[1:]:
        factor_of = factor_of * one(*cut)
    return factor_of


def length_profile(number_of, total, most, skew):
    weights = [(1 << 20) // math.isqrt(standing ** skew) + 1 for standing in range(2, number_of + 1)]
    spare, counts = total - most - (number_of - 1), [1] * (number_of - 1)
    while spare > 0:
        movable = [i for i in range(number_of - 1) if counts[i] < most]
        whole, budget = sum([weights[i] for i in movable]), spare
        for i in movable:
            extra = min(most - counts[i], max(1, budget * weights[i] // whole), spare)
            counts[i] = counts[i] + extra
            spare = spare - extra
    return np.array([most] + counts)


def ragged_sizes(stream_key, amount, total, limit, skew):
    if amount == 2:
        one = jax.random.randint(stream_key, (), max(1, total - limit), min(limit, total - 1) + 1)
        return jnp.stack([one, total - one])
    sizes = jnp.asarray(length_profile(amount, total, limit, skew), jnp.int32)
    couples = (amount - 1) // 2
    source_of, taker = sizes[1:1 + 2 * couples:2], sizes[2:2 + 2 * couples:2]
    room = jnp.minimum(source_of - 1, limit - taker)
    passed = jax.random.randint(jax.random.fold_in(stream_key, 1), (couples,), 0, 1 << 20) % (room + 1)
    sizes = sizes.at[1:1 + 2 * couples:2].set(source_of - passed).at[2:2 + 2 * couples:2].set(taker + passed)
    return sizes[jax.random.permutation(jax.random.fold_in(stream_key, 2), amount)]


def assign_block(rng, own, number, rows, number_of, top, reach, slope):
    order = jax.random.permutation(rng, number_of)
    packed, common = portions_of(number_of, rows * top, reach, slope, True), portions_of(number_of, rows * top, reach, slope, False)
    places = jnp.arange(number_of)

    def named(tallies, rotation):
        used = int((tallies > 0).sum())
        fixed = max(1, used // 4)
        shifted = fixed + (places - fixed + rotation * (used - fixed)) % max(1, number_of - fixed)
        return jnp.zeros((number_of,), jnp.int32).at[order[jnp.where(places < fixed, places, shifted)]].set(jnp.asarray(tallies, jnp.int32))

    tallies = jnp.where(number % 4 == 0, named(packed, number // 4), named(common, number - number // 4 - 1))
    mixed = jax.random.permutation(jax.random.fold_in(own, 3), number_of)
    giver, sink = mixed[0:number_of // 2 * 2:2], mixed[1:number_of // 2 * 2:2]
    slack = jnp.minimum(tallies[giver] - 1, reach - tallies[sink]) // 2
    slack = jnp.where((giver == order[0]) | (sink == order[0]) | (tallies[sink] == 0), 0, jnp.maximum(slack, 0))
    shifted = jax.random.randint(jax.random.fold_in(own, 4), (number_of // 2,), 0, 1 << 20) % (slack + 1)
    tallies = tallies.at[giver].add(-shifted).at[sink].add(shifted)
    items = jnp.searchsorted(jnp.cumsum(tallies), jnp.arange(rows * top), side="right").astype(jnp.int32)
    grid = items.reshape(top, rows).T
    grid = grid[jax.random.permutation(jax.random.fold_in(own, 1), rows)]
    rotation = jax.random.randint(jax.random.fold_in(own, 2), (rows, 1), 0, top)
    return jnp.take_along_axis(grid, (jnp.arange(top)[None, :] + rotation) % top, axis=1)


def portions_of(count, total, most, skew, full):
    portions = [(1 << 20) // math.isqrt(standing ** skew) + 1 for standing in range(1, count + 1)]
    largest = most if full else min(most, max(-(-total // count), total * portions[0] // sum(portions)))
    least = 1 if total - largest >= count - 1 else 0
    holding, spare = [largest] + [least] * (count - 1), total - largest - least * (count - 1)
    while spare > 0:
        candidates = [i for i in range(1, count) if holding[i] < largest] or [i for i in range(1, count) if holding[i] < most]
        whole, budget = sum([portions[i] for i in candidates]), spare
        for i in candidates:
            addition = min(most - holding[i], max(1, budget * portions[i] // whole), spare)
            holding[i] = holding[i] + addition
            spare = spare - addition
    return np.array(holding)


def normal_values(own_key, dims, spread, most, cuts=(), kind=jnp.bfloat16):
    entries = jax.random.normal(own_key, dims, jnp.float32) * spread
    if len(cuts) > 0:
        entries = steps_of(own_key, dims, cuts, -0.22, 0.18) * entries
    return jnp.clip(entries, min=-most, max=most).astype(kind)


def setup_inputs(seed: int = 0) -> dict:
    keys = jax.random.split(jax.random.key(seed), 20)
    tokens = normal_values(keys[0], (TOKEN_TOTAL, MODEL_WIDTH), 1.0, 6.0, ((0, 16),))
    cotangent = normal_values(keys[1], (TOKEN_TOTAL, MODEL_WIDTH), 1.0, 6.0, ((0, 16),))
    lengths = jax.vmap(lambda own: ragged_sizes(own, SEQS, GROUP, MAXLEN, 2))(jax.random.split(keys[2], GROUPS)).reshape((GROUPS, SEQS)).astype(jnp.int32)
    deal_order = jax.vmap(lambda own: jax.random.permutation(own, GROUP))(jax.random.split(keys[3], GROUPS)).reshape((GROUPS, GROUP)).astype(jnp.int32)
    routes_keys = jax.random.split(jax.random.fold_in(keys[4], 1), TOKEN_TOTAL // TOK_DEV)
    routes_turns = jax.random.permutation(jax.random.fold_in(keys[4], 3), TOKEN_TOTAL // TOK_DEV)
    routes = jax.vmap(lambda own, number: assign_block(jax.random.fold_in(keys[4], 2), own, number, TOK_DEV, EXPERTS, TOP, CAP, 1))(routes_keys, routes_turns).reshape((TOKEN_TOTAL, TOP))
    attn_gain = jnp.clip(1.0 + 0.18 * jax.random.normal(keys[5], (MODEL_WIDTH,), jnp.float32), 0.099609375, 1.8984375).astype(jnp.bfloat16)
    q_weight = normal_values(keys[6], (MODEL_WIDTH, H * (NOPE + ROPE)), MODEL_WIDTH ** -0.5, 0.125, ((0, 16), (1, 2)))
    kv_down = normal_values(keys[7], (MODEL_WIDTH, KV_RANK + ROPE), MODEL_WIDTH ** -0.5, 0.125, ((0, 16),))
    latent_gain = jnp.clip(1.0 + 0.18 * jax.random.normal(keys[8], (KV_RANK,), jnp.float32), 0.099609375, 1.8984375).astype(jnp.bfloat16)
    kv_up = normal_values(keys[9], (KV_RANK, H * (NOPE + VDIM)), KV_RANK ** -0.5, 0.25, ((0, 16), (1, 2)))
    out_weight = normal_values(keys[10], (H * VDIM, MODEL_WIDTH), (H * VDIM // 32) ** -0.5, 0.75, ((0, 2), (1, 16)))
    ffn_gain = jnp.clip(1.0 + 0.18 * jax.random.normal(keys[11], (MODEL_WIDTH,), jnp.float32), 0.099609375, 1.8984375).astype(jnp.bfloat16)
    router = normal_values(keys[12], (MODEL_WIDTH, EXPERTS), (0.5 * MODEL_WIDTH ** -0.5), 0.0625, ((0, 16),))
    shared_gate = normal_values(keys[13], (MODEL_WIDTH, FF_SH), MODEL_WIDTH ** -0.5, 0.125, ((0, 16), (1, 2)))
    shared_up = normal_values(keys[14], (MODEL_WIDTH, FF_SH), MODEL_WIDTH ** -0.5, 0.125, ((0, 16), (1, 2)))
    shared_down = normal_values(keys[15], (FF_SH, MODEL_WIDTH), FF_SH ** -0.5, 0.109375, ((0, 2), (1, 16)))
    expert_gate = normal_values(keys[16], (EXPERTS, MODEL_WIDTH, FF_EXP), MODEL_WIDTH ** -0.5, 0.125, ((0, 16), (2, 2)))
    expert_up = normal_values(keys[17], (EXPERTS, MODEL_WIDTH, FF_EXP), MODEL_WIDTH ** -0.5, 0.125, ((0, 16), (2, 2)))
    expert_down = normal_values(keys[18], (EXPERTS, FF_EXP, MODEL_WIDTH), (max(FF_EXP // 256, 1)) ** -0.5, 2.5, ((0, 16), (1, 2)))
    return {"tokens": tokens, "cotangent": cotangent, "lengths": lengths, "deal_order": deal_order, "routes": routes, "attn_gain": attn_gain, "q_weight": q_weight, "kv_down": kv_down, "latent_gain": latent_gain, "kv_up": kv_up, "out_weight": out_weight, "ffn_gain": ffn_gain, "router": router, "shared_gate": shared_gate, "shared_up": shared_up, "shared_down": shared_down, "expert_gate": expert_gate, "expert_up": expert_up, "expert_down": expert_down}


EPSILON = 1e-06
NEGATIVE = -1e+30
PRECISE = lax.Precision.HIGHEST

@jax.custom_vjp
def low(v):
    return lax.optimization_barrier(v.astype(jnp.bfloat16)).astype(jnp.float32)

@jax.custom_vjp
def low_back(v):
    return v

def low_keep(v):
    return (low(v), None)

def low_pass(kept, grad):
    return (grad,)

def back_keep(v):
    return (v, None)

def back_low(kept, grad):
    return (low(grad),)
low.defvjp(low_keep, low_pass)
low_back.defvjp(back_keep, back_low)

def matmul(left_in, right_in):
    return jnp.dot(left_in, right_in, precision=PRECISE, preferred_element_type=jnp.float32)

def rmsnorm(values, gain_vec):
    return values * lax.rsqrt(lax.optimization_barrier(jnp.mean(values * values, axis=-1, keepdims=True)) + EPSILON) * gain_vec

def gated_silu_product(gate_in, up_in):
    return jax.nn.silu(gate_in) * up_in

def rope_tables(position):
    frequency = jnp.exp(jnp.arange(ROPE // 2, dtype=jnp.float32) * (-2.0 * math.log(10000.0) / ROPE))
    angle_table = position.astype(jnp.float32)[:, None] * frequency[None, :]
    return (jnp.cos(angle_table), jnp.sin(angle_table))

def rotate(values, cos_table, sin_table):
    half_size = values.shape[-1] // 2
    first_half = values[..., :half_size]
    second_half = values[..., half_size:]
    return jnp.concatenate([first_half * cos_table - second_half * sin_table, first_half * sin_table + second_half * cos_table], axis=-1)

def places(lengths_row, order_row):
    doc_ends = jnp.cumsum(lengths_row).astype(jnp.int32)
    starts = doc_ends - lengths_row
    doc_ids = lax.optimization_barrier(jnp.sum((order_row[:, None] >= doc_ends[None, :]).astype(jnp.int32), axis=1))
    matched = doc_ids[:, None] == jnp.arange(lengths_row.shape[0], dtype=jnp.int32)[None, :]
    doc_start = lax.optimization_barrier(jnp.sum(jnp.where(matched, starts[None, :], 0), axis=1))
    return (doc_ids, order_row - doc_start)

def slot_lookup(routes):
    block_total = N_DP * N_CTX
    per_block = TOK_DEV * TOP
    flat_routes = routes.reshape(block_total, per_block)
    entry_hot = (flat_routes[:, :, None] == jnp.arange(EXPERTS, dtype=jnp.int32)[None, None, :]).astype(jnp.int32)
    slot_rank = lax.optimization_barrier(jnp.sum((jnp.cumsum(entry_hot, axis=1) - entry_hot) * entry_hot, axis=2))
    block_ids = jnp.arange(block_total, dtype=jnp.int32)[:, None]
    destination = flat_routes * (block_total * CAP) + block_ids * CAP + slot_rank
    slot_table = jnp.full((EXPERTS * block_total * CAP,), TOKEN_TOTAL * TOP, jnp.int32)
    slot_table = slot_table.at[destination.reshape(-1)].set(jnp.arange(TOKEN_TOTAL * TOP, dtype=jnp.int32))
    return slot_table.reshape(EXPERTS, block_total * CAP)

def expert(rows_in, gate_w, up_w, down_w):
    part_size = FF_EXP // N_TP
    summed = jnp.zeros(rows_in.shape, jnp.float32)
    for portion in range(N_TP):
        start_col = portion * part_size
        stop_col = start_col + part_size
        copied = low_back(rows_in)
        gate_pre = low_back(matmul(copied, gate_w[:, start_col:stop_col]))
        up_pre = low_back(matmul(copied, up_w[:, start_col:stop_col]))
        hidden = low(gated_silu_product(gate_pre, up_pre))
        summed = summed + low_back(low(matmul(hidden, down_w[start_col:stop_col])))
    return summed

def reference(tokens, cotangent, lengths, deal_order, routes, attn_gain, q_weight, kv_down, latent_gain, kv_up, out_weight, ffn_gain, router, shared_gate, shared_up, shared_down, expert_gate, expert_up, expert_down):
    doc_ids, position = jax.vmap(places)(lengths, deal_order)
    cos_table, sin_table = rope_tables(position.reshape(TOKEN_TOTAL))
    slot_table = slot_lookup(routes)
    scale_factor = (NOPE + ROPE) ** (-0.5)

    def attend(pieces):
        queries, keys_in, values_in, docs_in, pos_in = pieces
        raw_scores = low_back(jnp.einsum('qhd,khd->hqk', queries, keys_in, precision=PRECISE))
        allowed = (docs_in[:, None] == docs_in[None, :]) & (pos_in[None, :] <= pos_in[:, None])
        scores = jnp.where(allowed[None], raw_scores * scale_factor, NEGATIVE)
        highest = lax.optimization_barrier(jnp.max(scores, axis=-1, keepdims=True))
        exponentials = jnp.exp(scores - highest)
        probabilities = exponentials / lax.optimization_barrier(jnp.sum(exponentials, axis=-1, keepdims=True))
        return jnp.einsum('hqk,khd->qhd', low(probabilities), values_in, precision=PRECISE)

    def decoder_layer(input_rows, attention_scale, query_weight_whole, down_weight_whole, latent_norm_scale, up_weight_whole, output_weight_whole, feedforward_scale, router_weight_whole, shared_gate_whole, shared_up_whole, shared_down_whole, expert_gate_whole, expert_up_whole, expert_down_whole):
        normed_low = low(rmsnorm(input_rows, attention_scale))
        query_pre = low_back(matmul(normed_low, query_weight_whole)).reshape(TOKEN_TOTAL, H, NOPE + ROPE)
        query_low = low(jnp.concatenate([query_pre[..., :NOPE], rotate(query_pre[..., NOPE:], cos_table[:, None], sin_table[:, None])], axis=-1))
        latent_pre = low_back(matmul(normed_low, down_weight_whole))
        latent_low = low(rmsnorm(latent_pre[:, :KV_RANK], latent_norm_scale))
        rope_low = low(rotate(latent_pre[:, KV_RANK:], cos_table, sin_table))
        expanded = low(matmul(latent_low, up_weight_whole)).reshape(TOKEN_TOTAL, H, NOPE + VDIM)
        keys_all = jnp.concatenate([expanded[..., :NOPE], jnp.broadcast_to(rope_low[:, None, :], (TOKEN_TOTAL, H, ROPE))], axis=-1)
        values_all = expanded[..., NOPE:]
        grouped = lax.map(jax.checkpoint(attend), (query_low.reshape(N_DP, GROUP, H, NOPE + ROPE), keys_all.reshape(N_DP, GROUP, H, NOPE + ROPE), values_all.reshape(N_DP, GROUP, H, VDIM), doc_ids, position))
        attended = low(low_back(grouped.reshape(TOKEN_TOTAL, H * VDIM)))
        hidden_one = input_rows + low_back(matmul(attended, output_weight_whole))
        ffn_low = low(rmsnorm(hidden_one, feedforward_scale))
        router_probs = jax.nn.softmax(matmul(ffn_low, router_weight_whole), axis=-1)
        gate_values = jnp.take_along_axis(router_probs, routes, axis=1)
        shared_hidden = low(gated_silu_product(low_back(matmul(ffn_low, shared_gate_whole)), low_back(matmul(ffn_low, shared_up_whole))))
        shared_out = low_back(matmul(shared_hidden, shared_down_whole))
        padded_rows = jnp.concatenate([ffn_low, jnp.zeros((1, MODEL_WIDTH), jnp.float32)], axis=0)
        padded_gates = jnp.concatenate([gate_values.reshape(TOKEN_TOTAL * TOP), jnp.zeros((1,), jnp.float32)], axis=0)

        def expert_update(routed_tokens, pieces):
            index_row, gate_w, up_w, down_w = pieces
            token_index = index_row // TOP
            produced = expert(padded_rows[token_index], gate_w, up_w, down_w)
            weighted = produced * padded_gates[index_row][:, None]
            return (routed_tokens.at[token_index].add(weighted), None)
        routed_tokens, discarded_value = lax.scan(jax.checkpoint(expert_update), jnp.zeros((TOKEN_TOTAL + 1, MODEL_WIDTH), jnp.float32), (slot_table, expert_gate_whole, expert_up_whole, expert_down_whole))
        return hidden_one + shared_out + routed_tokens[:TOKEN_TOTAL]
    weights_in = tuple((array_in.astype(jnp.float32) for array_in in (attn_gain, q_weight, kv_down, latent_gain, kv_up, out_weight, ffn_gain, router, shared_gate, shared_up, shared_down, expert_gate, expert_up, expert_down)))
    output, pullback = jax.vjp(decoder_layer, tokens.astype(jnp.float32), *weights_in)
    gradients = pullback(cotangent.astype(jnp.float32))
    return (output.astype(jnp.bfloat16), gradients[0], gradients[1], gradients[2], gradients[3], gradients[4], gradients[5], gradients[6], gradients[7], gradients[8], gradients[9], gradients[10], gradients[11], gradients[12], gradients[13], gradients[14])
```

```python
import functools
import math

import jax
import jax.numpy as jnp
from jax import lax
from jax.sharding import PartitionSpec as P

NOPE = 128
ROPE = 64
VDIM = 128
KV_RANK = 512
LANES = 128

EPSILON = 1e-06
NEGATIVE = -1e30
PRECISE = lax.Precision.HIGHEST
BF = jnp.bfloat16
F32 = jnp.float32
GRID = ("dp", "ctx")


def rmsnorm(values, gain_vec):
    return (
        values * lax.rsqrt(jnp.mean(values * values, axis=-1, keepdims=True) + EPSILON) * gain_vec
    )


def rope_tables(position):
    frequency = jnp.exp(
        jnp.arange(ROPE // 2, dtype=F32) * (-2.0 * math.log(10000.0) / ROPE)
    )
    angle_table = position.astype(F32)[:, None] * frequency[None, :]
    return (jnp.cos(angle_table), jnp.sin(angle_table))


def rotate(values, cos_table, sin_table):
    half_size = values.shape[-1] // 2
    first_half = values[..., :half_size]
    second_half = values[..., half_size:]
    return jnp.concatenate(
        [
            first_half * cos_table - second_half * sin_table,
            first_half * sin_table + second_half * cos_table,
        ],
        axis=-1,
    )


def unrotate(values, cos_table, sin_table):
    return rotate(values, cos_table, -sin_table)


def places(lengths_row, order_row):
    doc_ends = jnp.cumsum(lengths_row)
    starts = doc_ends - lengths_row
    doc_ids = jnp.sum((order_row[:, None] >= doc_ends[None, :]).astype(jnp.int32), axis=1)
    matched = doc_ids[:, None] == jnp.arange(lengths_row.shape[0], dtype=jnp.int32)[None, :]
    doc_start = jnp.sum(jnp.where(matched, starts[None, :], 0), axis=1)
    return (doc_ids, order_row - doc_start)


def dot(left, right):
    return jnp.dot(left, right, preferred_element_type=F32)


def dot_nt(left, right):
    return lax.dot_general(left, right, (((1,), (1,)), ((), ())), preferred_element_type=F32)


def dot_tn(left, right):
    return lax.dot_general(left, right, (((0,), (0,)), ((), ())), preferred_element_type=F32)


def two_parts(values):
    high = lax.reduce_precision(values, 8, 7)
    return high.astype(BF), (values - high).astype(BF)


def body(
    n_dp,
    n_ctx,
    tokens,
    cotangent,
    lengths,
    deal_order,
    routes,
    attn_gain,
    q_weight,
    kv_down,
    latent_gain,
    kv_up,
    out_weight,
    ffn_gain,
    router,
    shared_gate,
    shared_up,
    shared_down,
    expert_gate,
    expert_up,
    expert_down,
):
    rows, width = tokens.shape
    half = rows // 2
    top = routes.shape[1]
    experts = router.shape[1]
    blocks = n_dp * n_ctx
    band = width // blocks
    slots = 4 * rows * top // (3 * experts) // 2
    z = lax.axis_index("dp")
    c = lax.axis_index("ctx")
    t = lax.axis_index("tp")
    expert_id = z * n_ctx + c
    width_qk = NOPE + ROPE
    width_kv = NOPE + VDIM
    scale_factor = width_qk ** (-0.5)
    heads = q_weight.shape[1] // width_qk // n_ctx
    pack = rows * n_ctx

    def across(x, j):
        return lax.ppermute(x, "ctx", [(i, i ^ j) for i in range(n_ctx)])

    def swap(x):
        return lax.ppermute(x, "tp", [(0, 1), (1, 0)])

    def hop(x):
        return lax.ppermute(x, "dp", [(i, (i + 1) % n_dp) for i in range(n_dp)])

    def own_half(x):
        return lax.dynamic_slice_in_dim(x, t * half, half)

    def both_halves(x):
        other = swap(x)
        first = t == 0
        return jnp.concatenate([jnp.where(first, x, other), jnp.where(first, other, x)], axis=0)

    def gather_pack(x):
        near = jnp.concatenate([x] + [across(x, j) for j in range(1, n_ctx)], axis=0)
        return jnp.concatenate([near, swap(near)], axis=0)

    def scatter_pack(y):
        middle = y.shape[0] // 2
        near = y[:middle] + swap(y[middle:].astype(BF)).astype(F32)
        near = near.reshape(n_ctx, half, y.shape[1])
        total = near[0]
        for j in range(1, n_ctx):
            total = total + across(near[j].astype(BF), j).astype(F32)
        return total

    q_cols, out_cols = heads * width_qk, heads * VDIM
    up_cols = heads * width_kv
    up_rows = kv_up.shape[0]
    folds = up_cols // LANES

    def head_pieces(q, out_t, up):
        folded = up.reshape(up_rows, n_ctx, folds, LANES).transpose(1, 2, 0, 3)
        folded = folded.reshape(n_ctx, folds * up_rows, LANES)
        return jnp.concatenate(
            [
                q.reshape(band, n_ctx, q_cols).transpose(1, 0, 2),
                out_t.reshape(band, n_ctx, out_cols).transpose(1, 0, 2),
                folded,
            ],
            axis=2,
        )

    small = jnp.concatenate([attn_gain, ffn_gain, latent_gain, router.reshape(band * experts)])
    small_all = lax.all_gather(small, GRID, axis=0, tiled=False)
    attn_gain_all = small_all[:, :band].reshape(width).astype(F32)
    ffn_gain_all = small_all[:, band : 2 * band].reshape(width).astype(F32)
    latent_cols = latent_gain.shape[0]
    latent_gain_all = (
        small_all[:, 2 * band : 2 * band + latent_cols].reshape(KV_RANK).astype(F32)
    )
    router_all = small_all[:, 2 * band + latent_cols :].reshape(width, experts)

    down_half = lax.dynamic_slice_in_dim(kv_down, t * (band // 2), band // 2)
    down_all = lax.all_gather(down_half, ("dp", "ctx", "tp"), axis=0, tiled=True)

    head_send = head_pieces(q_weight, out_weight.T, kv_up)
    head_mine = lax.all_to_all(head_send, "ctx", split_axis=0, concat_axis=0, tiled=True)
    head_all = lax.all_gather(head_mine, "dp", axis=0, tiled=True).reshape(width, -1)
    q_mine = head_all[:, :q_cols]
    out_mine = head_all[:, q_cols : q_cols + out_cols]
    up_mine = (
        head_all[:, q_cols + out_cols :]
        .reshape(blocks, folds, up_rows, LANES)
        .transpose(0, 2, 1, 3)
        .reshape(KV_RANK, up_cols)
    )

    hidden_units = shared_gate.shape[1] // n_dp
    shared_send = jnp.concatenate(
        [
            w.reshape(band, n_dp, hidden_units).transpose(1, 0, 2)
            for w in (shared_gate, shared_up, shared_down.T)
        ],
        axis=2,
    )
    shared_part = lax.all_to_all(shared_send, "dp", split_axis=0, concat_axis=0, tiled=True)
    shared_all = lax.all_gather(shared_part, "ctx", axis=1, tiled=True).reshape(width, -1)
    shared_in = shared_all[:, : 2 * hidden_units]
    shared_out_t = shared_all[:, 2 * hidden_units :]

    order_index = (c ^ jnp.arange(n_ctx))[None, :] * 2 + (t ^ jnp.arange(2))[:, None]
    order_row = deal_order[0].reshape(n_ctx * 2, half)[order_index.reshape(-1)].reshape(pack)
    docs, pos = places(lengths[0], order_row)
    cos_table, sin_table = rope_tables(pos)
    token_pack = gather_pack(own_half(tokens))
    normed_low = rmsnorm(token_pack.astype(F32), attn_gain_all).astype(BF)
    query_pre = dot(normed_low, q_mine).reshape(pack, heads, width_qk)
    query_low = jnp.concatenate(
        [
            query_pre[..., :NOPE],
            rotate(query_pre[..., NOPE:], cos_table[:, None], sin_table[:, None]),
        ],
        axis=-1,
    ).astype(BF)
    latent_pre = dot(normed_low, down_all)
    latent_low = rmsnorm(latent_pre[:, :KV_RANK], latent_gain_all).astype(BF)
    rope_low = rotate(latent_pre[:, KV_RANK:], cos_table, sin_table).astype(BF)
    expanded = dot(latent_low, up_mine).astype(BF).reshape(pack, heads, width_kv)
    keys = jnp.concatenate(
        [expanded[..., :NOPE], jnp.broadcast_to(rope_low[:, None, :], (pack, heads, ROPE))],
        axis=-1,
    )
    values = expanded[..., NOPE:]
    allowed = (docs[:, None] == docs[None, :]) & (pos[None, :] <= pos[:, None])

    def scores_of():
        raw = jnp.einsum("qhd,khd->hqk", query_low, keys, preferred_element_type=F32)
        return jnp.where(allowed[None], raw * scale_factor, NEGATIVE)

    scores = scores_of()
    highest = jnp.max(scores, axis=-1, keepdims=True)
    exponentials = jnp.exp(scores - highest)
    totals = jnp.sum(exponentials, axis=-1, keepdims=True)
    log_totals = highest + jnp.log(totals)
    attended = (
        jnp.einsum(
            "hqk,khd->qhd",
            (exponentials / totals).astype(BF),
            values,
            preferred_element_type=F32,
        )
        .reshape(pack, heads * VDIM)
        .astype(BF)
    )
    own_tokens = own_half(tokens).astype(F32)
    hidden_one = own_tokens + scatter_pack(dot_nt(attended, out_mine))

    own_cot = own_half(cotangent)
    expert_row = jnp.arange(experts, dtype=jnp.int32)
    hot = jnp.sum((routes[:, :, None] == expert_row[None, None, :]).astype(BF), axis=1)
    row_index = jnp.arange(rows)
    earlier = (row_index[:, None] >= row_index[None, :]).astype(BF)
    rank = dot(earlier, hot) * hot.astype(F32)

    def column(x):
        ring = [x]
        for _ in range(n_dp - 1):
            ring.append(hop(ring[-1]))
        ring = jnp.stack(ring)
        return jnp.concatenate([ring, swap(ring)], axis=1)

    cot_column = column(
        jnp.concatenate(
            [own_cot, own_half(rank).astype(BF), jnp.zeros((half, LANES - experts), BF)], axis=1
        )
    )
    pick = (
        expert_row[:, None] == (z * n_ctx + (c ^ jnp.arange(n_ctx, dtype=jnp.int32)))[None, :]
    ).astype(BF)
    wanted = jnp.einsum(
        "kre,ej->kjr",
        cot_column[:, :, width : width + experts],
        pick,
        preferred_element_type=F32,
    )
    slot_number = (t * slots + 1 + jnp.arange(slots)).astype(F32)
    choose = (wanted[:, :, None, :] == slot_number[None, None, :, None]).astype(BF)
    choose = choose.reshape(n_dp, n_ctx * slots, rows)

    def dispatch(col):
        picked = jnp.einsum("ksr,krw->ksw", choose, col, preferred_element_type=F32).astype(BF)
        picked = picked.reshape(n_dp, n_ctx, slots, -1).transpose(1, 0, 2, 3)
        picked = picked.reshape(n_ctx, n_dp * slots, -1)
        near = [picked[0]] + [across(picked[j], j) for j in range(1, n_ctx)]
        near = jnp.concatenate(near, axis=0)
        return jnp.concatenate([near, swap(near)], axis=0)

    def give_back(rows_out):
        low = rows_out.astype(BF).reshape(n_ctx, n_dp * slots, -1)
        near = jnp.stack([low[0]] + [across(low[j], j) for j in range(1, n_ctx)])
        near = near.reshape(n_ctx, n_dp, slots, -1).transpose(1, 0, 2, 3)
        return near.reshape(n_dp, n_ctx * slots, -1)

    def over_tp(x):
        middle = x.shape[0] // 2
        return x[:middle] + swap(x[middle:].astype(BF)).astype(F32)

    def ring_sum(part):
        total = None
        for k in range(1, n_dp + 1):
            col = part(k % n_dp)
            near = col[:half] + swap(col[half:].astype(BF)).astype(F32)
            total = near if total is None else hop(total.astype(BF)).astype(F32) + near
        return total

    cot_rows = dispatch(cot_column[:, :, :width])
    gate_w, up_w, down_w = expert_gate[0], expert_up[0], expert_down[0]
    back_hidden = dot_nt(cot_rows, down_w)
    cot_flat = cot_column[:, :, :width].reshape(n_dp * rows, width)
    back_shared = dot(cot_flat, shared_out_t)

    ffn_normed, ffn_norm_back = jax.vjp(rmsnorm, hidden_one, ffn_gain_all)
    ffn_low = ffn_normed.astype(BF)
    router_probs = jax.nn.softmax(dot(ffn_low, router_all), axis=-1)
    probs_high, probs_low = two_parts(router_probs)
    spare = jnp.zeros((half, LANES - 2 * experts), BF)
    ffn_column = column(jnp.concatenate([ffn_low, probs_high, probs_low, spare], axis=1))
    ffn_rows = dispatch(ffn_column)
    expert_hot = (expert_row == expert_id).astype(F32)
    lanes = ffn_rows[:, width : width + 2 * experts].astype(F32)
    gate = jnp.sum(
        (lanes[:, :experts] + lanes[:, experts:]) * expert_hot[None, :], axis=1, keepdims=True
    )
    x_rows = ffn_rows[:, :width]
    gate_pre = dot(x_rows, gate_w)
    up_pre = dot(x_rows, up_w)
    sig = jax.nn.sigmoid(gate_pre)
    act = gate_pre * sig
    hidden = act * up_pre
    gated_hidden = (gate * hidden).astype(BF)
    back_gate = jnp.sum(hidden * back_hidden, axis=1, keepdims=True)
    scaled_back = gate * back_hidden
    back_up_pre = (scaled_back * act).astype(BF)
    back_gate_pre = (scaled_back * up_pre * sig * (1.0 + gate_pre * (1.0 - sig))).astype(BF)
    back_rows = dot_nt(back_gate_pre, gate_w) + dot_nt(back_up_pre, up_w)

    x_flat = ffn_column[:, :, :width].reshape(n_dp * rows, width)
    shared_pre = dot(x_flat, shared_in)
    s_gate, s_up = shared_pre[:, :hidden_units], shared_pre[:, hidden_units:]
    s_sig = jax.nn.sigmoid(s_gate)
    s_act = s_gate * s_sig
    shared_hidden = (s_act * s_up).astype(BF)
    back_shared_pre = jnp.concatenate(
        [
            back_shared * s_up * s_sig * (1.0 + s_gate * (1.0 - s_sig)),
            back_shared * s_act,
        ],
        axis=1,
    ).astype(BF)
    shared_hidden_of = shared_hidden.reshape(n_dp, rows, hidden_units)
    back_shared_of = back_shared_pre.reshape(n_dp, rows, 2 * hidden_units)

    middle = back_gate.shape[0] // 2
    gate_total = back_gate[:middle] + swap(back_gate[middle:])
    gate_high, gate_low = two_parts(gate_total * expert_hot[None, :])
    back_near = jnp.concatenate(
        [
            over_tp(back_rows).astype(BF),
            gate_high,
            gate_low,
            jnp.zeros((middle, LANES - 2 * experts), BF),
        ],
        axis=1,
    )
    back_returned = give_back(back_near)

    def back_part(k):
        shared = dot_nt(back_shared_of[k], shared_in)
        return dot_tn(choose[k], back_returned[k]) + jnp.pad(shared, ((0, 0), (0, LANES)))

    back_ffn = ring_sum(back_part)
    back_probs = (
        back_ffn[:, width : width + experts] + back_ffn[:, width + experts : width + 2 * experts]
    )
    back_logits = router_probs * (
        back_probs - jnp.sum(router_probs * back_probs, axis=-1, keepdims=True)
    )
    back_ffn_normed = back_ffn[:, :width] + jnp.dot(
        back_logits, router_all.astype(F32).T, precision=PRECISE
    )
    grad_router = jnp.dot(ffn_low.astype(F32).T, back_logits, precision=PRECISE)
    back_hidden_one, grad_ffn_gain = ffn_norm_back(back_ffn_normed)
    back_hidden_one = back_hidden_one + own_cot.astype(F32)

    out_returned = give_back(over_tp(dot(gated_hidden, down_w)))

    def out_part(k):
        return dot_tn(choose[k], out_returned[k]) + dot_nt(shared_hidden_of[k], shared_out_t)

    output = both_halves((hidden_one + ring_sum(out_part)).astype(BF))

    grad_egate = dot_tn(x_rows, back_gate_pre)
    grad_eup = dot_tn(x_rows, back_up_pre)
    grad_edown = dot_tn(gated_hidden, cot_rows)
    grad_shared = jnp.concatenate(
        [dot_tn(x_flat, back_shared_pre), dot_tn(cot_flat, shared_hidden)], axis=1
    ).astype(BF)
    grad_shared = lax.psum_scatter(
        grad_shared.reshape(n_dp, n_ctx * band, 3 * hidden_units),
        "ctx",
        scatter_dimension=1,
        tiled=True,
    )
    grad_shared = lax.all_to_all(grad_shared, "dp", split_axis=0, concat_axis=0, tiled=True)
    grad_shared = grad_shared.astype(F32)
    grad_sgate, grad_sup, grad_sdown = (
        grad_shared[:, :, i * hidden_units : (i + 1) * hidden_units]
        .transpose(1, 0, 2)
        .reshape(band, n_dp * hidden_units)
        for i in range(3)
    )
    early = jnp.concatenate([grad_router, grad_ffn_gain[:, None]], axis=1)
    early = lax.psum_scatter(early + swap(early), GRID, scatter_dimension=0, tiled=True)

    back_pack = gather_pack(back_hidden_one.astype(BF))
    back_attended = dot(back_pack, out_mine).astype(BF)
    grad_out_t = dot_tn(back_pack, attended)
    back_heads = back_attended.reshape(pack, heads, VDIM)
    probabilities = jnp.exp(scores_of() - log_totals)
    back_prob = jnp.einsum("qhd,khd->hqk", back_heads, values, preferred_element_type=F32)
    inner_sum = jnp.sum(probabilities * back_prob, axis=-1, keepdims=True)
    back_raw = (probabilities * (back_prob - inner_sum) * scale_factor).astype(BF)
    back_queries = jnp.einsum("hqk,khd->qhd", back_raw, keys, preferred_element_type=F32)
    back_keys = jnp.einsum("hqk,qhd->khd", back_raw, query_low, preferred_element_type=F32)
    back_values = jnp.einsum(
        "hqk,qhd->khd", probabilities.astype(BF), back_heads, preferred_element_type=F32
    )
    back_query_pre = (
        jnp.concatenate(
            [
                back_queries[..., :NOPE],
                unrotate(back_queries[..., NOPE:], cos_table[:, None], sin_table[:, None]),
            ],
            axis=-1,
        )
        .reshape(pack, q_cols)
        .astype(BF)
    )
    back_expanded = (
        jnp.concatenate([back_keys[..., :NOPE], back_values], axis=-1)
        .reshape(pack, up_cols)
        .astype(BF)
    )
    back_sum = scatter_pack(
        jnp.concatenate(
            [
                dot_nt(back_query_pre, q_mine),
                dot_nt(back_expanded, up_mine),
                jnp.sum(back_keys[..., NOPE:], axis=1),
            ],
            axis=1,
        )
    )
    own_latent = latent_pre[:half, :KV_RANK]
    back_latent_pre, grad_latent_gain = jax.vjp(rmsnorm, own_latent, latent_gain_all)[1](
        back_sum[:, width : width + KV_RANK]
    )
    back_down = jnp.concatenate(
        [
            back_latent_pre,
            unrotate(back_sum[:, width + KV_RANK :], cos_table[:half], sin_table[:half]),
        ],
        axis=1,
    ).astype(BF)
    back_normed = back_sum[:, :width] + dot_nt(back_down, down_all)
    back_inputs, grad_attn_gain = jax.vjp(rmsnorm, own_tokens, attn_gain_all)[1](back_normed)
    input_grad = both_halves(back_hidden_one + back_inputs)

    grad_heads = jnp.concatenate(
        [
            dot_tn(normed_low, back_query_pre),
            grad_out_t,
            dot_tn(latent_low, back_expanded)
            .reshape(blocks, up_rows, folds, LANES)
            .transpose(0, 2, 1, 3)
            .reshape(width, LANES),
        ],
        axis=1,
    ).astype(BF)
    grad_heads = lax.psum_scatter(grad_heads, "dp", scatter_dimension=0, tiled=True)
    grad_heads = lax.all_to_all(
        grad_heads.reshape(n_ctx, band, -1), "ctx", split_axis=0, concat_axis=0, tiled=True
    ).astype(F32)
    grad_q = grad_heads[:, :, :q_cols].transpose(1, 0, 2).reshape(band, n_ctx * q_cols)
    grad_out = (
        grad_heads[:, :, q_cols : q_cols + out_cols]
        .transpose(0, 2, 1)
        .reshape(n_ctx * out_cols, band)
    )
    grad_up = (
        grad_heads[:, :, q_cols + out_cols :]
        .reshape(n_ctx, folds, up_rows, LANES)
        .transpose(2, 0, 1, 3)
        .reshape(up_rows, n_ctx * up_cols)
    )
    back_down_pack = gather_pack(back_down)
    normed_band = lax.dynamic_slice_in_dim(
        normed_low.reshape(pack, n_dp, n_ctx * band), c * band, band, axis=2
    ).reshape(pack, n_dp * band)
    grad_down = lax.psum_scatter(
        dot_tn(normed_band, back_down_pack), "dp", scatter_dimension=0, tiled=True
    )
    late = jnp.concatenate(
        [grad_attn_gain.reshape(blocks, band), grad_latent_gain.reshape(blocks, latent_cols)],
        axis=1,
    )
    late = jnp.sum(
        lax.all_to_all(late + swap(late), GRID, split_axis=0, concat_axis=0, tiled=True), axis=0
    )
    return (
        output,
        input_grad,
        late[:band],
        grad_q,
        grad_down,
        late[band:],
        grad_up,
        grad_out,
        early[:, experts],
        early[:, :experts],
        grad_sgate,
        grad_sup,
        grad_sdown.T,
        grad_egate[None],
        grad_eup[None],
        grad_edown[None],
    )


def solution(mesh):
    n_dp, n_ctx = mesh.shape["dp"], mesh.shape["ctx"]
    ins = (
        P(GRID, None),
        P(GRID, None),
        P("dp", None),
        P("dp", None),
        P(GRID, None),
        P(GRID),
        P(GRID, "tp"),
        P(GRID, None),
        P(GRID),
        P(GRID, "tp"),
        P("tp", GRID),
        P(GRID),
        P(GRID, None),
        P(GRID, "tp"),
        P(GRID, "tp"),
        P("tp", GRID),
        P(GRID, None, "tp"),
        P(GRID, None, "tp"),
        P(GRID, "tp", None),
    )
    outs = (
        P(GRID, None),
        P(GRID, None),
        P(GRID),
        P(GRID, "tp"),
        P(GRID, None),
        P(GRID),
        P(GRID, "tp"),
        P("tp", GRID),
        P(GRID),
        P(GRID, None),
        P(GRID, "tp"),
        P(GRID, "tp"),
        P("tp", GRID),
        P(GRID, None, "tp"),
        P(GRID, None, "tp"),
        P(GRID, "tp", None),
    )
    return jax.shard_map(
        functools.partial(body, n_dp, n_ctx),
        mesh=mesh,
        in_specs=ins,
        out_specs=outs,
        check_vma=False,
    )
```

```python
import functools
import math

import jax
import jax.numpy as jnp
from jax import lax
from jax.experimental import pallas as pl
from jax.experimental.pallas import tpu as pltpu
from jax.sharding import PartitionSpec as P

NOPE = 128
ROPE = 64
VDIM = 128
KV_RANK = 512
LANES = 128

EPSILON = 1e-06
NEGATIVE = -1e30
PRECISE = lax.Precision.HIGHEST
BF = jnp.bfloat16
F32 = jnp.float32
GRID = ("dp", "ctx")


def rmsnorm(values, gain_vec):
    return (
        values * lax.rsqrt(jnp.mean(values * values, axis=-1, keepdims=True) + EPSILON) * gain_vec
    )


def rope_tables(position):
    frequency = jnp.exp(
        jnp.arange(ROPE // 2, dtype=F32) * (-2.0 * math.log(10000.0) / ROPE)
    )
    angle_table = position.astype(F32)[:, None] * frequency[None, :]
    return (jnp.cos(angle_table), jnp.sin(angle_table))


def rotate(values, cos_table, sin_table):
    half_size = values.shape[-1] // 2
    first_half = values[..., :half_size]
    second_half = values[..., half_size:]
    return jnp.concatenate(
        [
            first_half * cos_table - second_half * sin_table,
            first_half * sin_table + second_half * cos_table,
        ],
        axis=-1,
    )


def unrotate(values, cos_table, sin_table):
    return rotate(values, cos_table, -sin_table)


def places(lengths_row, order_row):
    doc_ends = jnp.cumsum(lengths_row)
    starts = doc_ends - lengths_row
    doc_ids = jnp.sum((order_row[:, None] >= doc_ends[None, :]).astype(jnp.int32), axis=1)
    matched = doc_ids[:, None] == jnp.arange(lengths_row.shape[0], dtype=jnp.int32)[None, :]
    doc_start = jnp.sum(jnp.where(matched, starts[None, :], 0), axis=1)
    return (doc_ids, order_row - doc_start)


def dot(left, right):
    return jnp.dot(left, right, preferred_element_type=F32)


def dot_nt(left, right):
    return lax.dot_general(left, right, (((1,), (1,)), ((), ())), preferred_element_type=F32)


def dot_tn(left, right):
    return lax.dot_general(left, right, (((0,), (0,)), ((), ())), preferred_element_type=F32)


def two_parts(values):
    high = lax.reduce_precision(values, 8, 7)
    return high.astype(BF), (values - high).astype(BF)


TILE = 512


def whole(shape):
    return pl.BlockSpec(shape, lambda *_: (0,) * len(shape))


def scalar_spec():
    return pl.BlockSpec(memory_space=pltpu.SMEM)


def like(shape, dtype):
    return jax.ShapeDtypeStruct(shape, dtype)


def launch(kernel, name, args, in_specs, outs, out_specs, flops, grid=(1,), scratch=()):
    moved = sum(math.prod(a.shape) * a.dtype.itemsize for a in (*args, *outs))
    return pl.pallas_call(
        kernel,
        grid=grid,
        in_specs=in_specs,
        out_specs=out_specs,
        out_shape=outs,
        scratch_shapes=scratch,
        name=name,
        cost_estimate=pl.CostEstimate(flops=flops, bytes_accessed=moved, transcendentals=0),
    )(*args)


def spans(total, step):
    return [slice(lo, min(lo + step, total)) for lo in range(0, total, step)]


def fill(ref, parts, cols):
    row = 0
    for part in parts:
        size = part.shape[-2]
        value = part[..., cols]
        ref[row : row + size, :] = value.reshape(size, value.shape[-1])
        row += size


def drain(outs, value, cols):
    row = 0
    for out in outs:
        size = out.shape[0]
        out[:, cols] = value[row : row + size]
        row += size


def slot_places(ids, slots, ranks):
    plane = ids.shape[0] - 1
    lane = lax.broadcasted_iota(jnp.int32, (8, LANES), 1)
    sub = lax.broadcasted_iota(jnp.int32, (8, LANES), 0)
    found = jnp.zeros((8, LANES), F32)
    for j in range(plane):
        found = jnp.where((sub == j) & (lane == ids[j]), 1.0, found)
    return found.astype(BF), ids[plane].astype(F32), plane


def within(number, first, slots, j):
    place = number - first
    return jnp.where((place >= 0) & (place < slots), place + j * slots, -1.0)


def choose_rows(ids, slots, ranks):
    found, first, plane = slot_places(ids, slots, ranks)
    numbers = dot_nt(found, ranks)
    total, rows = plane * slots, ranks.shape[0]
    place = lax.broadcasted_iota(jnp.int32, (total, rows), 0).astype(F32)
    chosen = jnp.zeros((total, rows), F32)
    for j in range(plane):
        chosen = jnp.where(place == within(numbers[j : j + 1, :], first, slots, j), 1.0, chosen)
    return chosen.astype(BF)


def choose_slots(ids, slots, ranks):
    found, first, plane = slot_places(ids, slots, ranks)
    numbers = dot_nt(ranks, found)
    total, rows = plane * slots, ranks.shape[0]
    place = lax.broadcasted_iota(jnp.int32, (rows, total), 1).astype(F32)
    chosen = jnp.zeros((rows, total), F32)
    for j in range(plane):
        chosen = jnp.where(place == within(numbers[:, j : j + 1], first, slots, j), 1.0, chosen)
    return chosen.astype(BF)


def pick_kernel(slots, ids, rank_a, rank_b, a, b, *outs_scratch):
    outs, (ranks, rows) = outs_scratch[:-2], outs_scratch[-2:]
    fill(ranks, (rank_a, rank_b), slice(None))
    fill(rows, (a, b), slice(0, rows.shape[1]))
    choose = choose_rows(ids, slots, ranks[...])
    for cols in spans(rows.shape[1], TILE):
        drain(outs, dot(choose, rows[:, cols]).astype(BF), cols)


def rank_spec(half, width):
    return pl.BlockSpec((half, LANES), lambda *_: (0, width // LANES))


def pick_rows(ids, slots, ranked, a, b, width, cols, parts):
    half = a.shape[0]
    total = (ids.shape[0] - 1) * slots
    outs = [like((total // parts, cols), BF)] * parts
    return launch(
        functools.partial(pick_kernel, slots),
        "pick_rows",
        (ids, *ranked, a, b),
        [scalar_spec()] + [rank_spec(half, width)] * 2 + [whole((half, cols))] * 2,
        outs,
        [whole(o.shape) for o in outs],
        4 * total * half * cols,
        scratch=[pltpu.VMEM((2 * half, LANES), BF), pltpu.VMEM((2 * half, cols), BF)],
    )


def cot_kernel(count, *refs):
    parts, (weight, back, rows) = refs[:count], refs[count:]
    fill(rows, parts, slice(None))
    for cols in spans(weight.shape[0], 256):
        back[:, cols] = dot_nt(rows[...], weight[cols, :])


def cot_product(parts, weight):
    total = sum(p.shape[0] for p in parts)
    units, width = weight.shape
    outs = [like((total, units), F32), like((total, width), BF)]
    return launch(
        functools.partial(cot_kernel, len(parts)),
        "cot_product",
        (*parts, weight),
        [whole(p.shape) for p in parts] + [whole(weight.shape)],
        outs,
        [whole(o.shape) for o in outs],
        2 * total * units * width,
    )


def cot_shared_kernel(count, *refs):
    parts, weight, outs = refs[:count], refs[count], refs[count + 1 :]
    half = parts[0].shape[0]
    for k, part in enumerate(parts):
        row = (k % 2) * half
        outs[k // 2][row : row + half, :] = dot(part[...], weight[...])


def cot_shared(pairs, weight):
    parts = [x for pair in pairs for x in pair]
    half = parts[0].shape[0]
    width, units = weight.shape
    outs = [like((2 * half, units), F32)] * len(pairs)
    return launch(
        functools.partial(cot_shared_kernel, len(parts)),
        "cot_shared",
        (*parts, weight),
        [whole((half, width))] * len(parts) + [whole(weight.shape)],
        outs,
        [whole(o.shape) for o in outs],
        2 * len(parts) * half * units * width,
    )


def lane_masks(first, experts):
    lane = lax.broadcasted_iota(jnp.int32, (1, LANES), 1)
    return lane == first, lane == first + experts


def split_lanes(masks, value):
    high = value.astype(BF).astype(F32)
    return jnp.where(masks[0], high, jnp.where(masks[1], value - high, 0.0))


def expert_kernel(count, experts, first, *refs):
    parts = refs[:count]
    back, gate_w, up_w, down_w, x, back_gate, back_up, gated, near, near_out, far = refs[
        count : count + 11
    ]
    gate_s, sum_s, acc, acc_out = refs[count + 11 :]
    step = pl.program_id(0)
    width = gate_w.shape[1]
    middle = near.shape[0]
    masks = lane_masks(first[0], experts)

    @pl.when(step == 0)
    def _():
        fill(x, parts, slice(0, width))
        row = 0
        for part in parts:
            size = part.shape[0]
            lanes = part[:, width:].astype(F32)
            gate = jnp.sum(jnp.where(masks[0] | masks[1], lanes, 0.0), axis=1, keepdims=True)
            gate_s[row : row + size, :] = jnp.broadcast_to(gate, (size, LANES))
            row += size
        sum_s[...] = jnp.zeros_like(sum_s)

    rows = x[...]
    gate_pre = dot_nt(rows, gate_w[...])
    up_pre = dot_nt(rows, up_w[...])
    gate = gate_s[:, :1]
    back_hidden = back[...]
    sig = jax.nn.sigmoid(gate_pre)
    act = gate_pre * sig
    hidden = act * up_pre
    gated[...] = (gate * hidden).astype(BF)
    sum_s[...] += jnp.broadcast_to(
        jnp.sum(hidden * back_hidden, axis=1, keepdims=True), sum_s.shape
    )
    scaled = gate * back_hidden
    back_up[...] = (scaled * act).astype(BF)
    back_gate[...] = (scaled * up_pre * sig * (1.0 + gate_pre * (1.0 - sig))).astype(BF)
    for cols in spans(width, TILE):
        part = dot(back_gate[...], gate_w[:, cols]) + dot(back_up[...], up_w[:, cols])
        part_out = dot(gated[...], down_w[:, cols])

        @pl.when(step == 0)
        def _():
            acc[:, cols] = part
            acc_out[:, cols] = part_out

        @pl.when(step > 0)
        def _():
            acc[:, cols] += part
            acc_out[:, cols] += part_out

    @pl.when(step == pl.num_programs(0) - 1)
    def _():
        near_out[...] = acc_out[:middle, :].astype(BF)
        near[:, :width] = acc[:middle, :]
        near[:, width:] = jnp.where(masks[0], sum_s[:middle, :], 0.0)
        far[:, :width] = acc_out[middle:, :].astype(BF)
        far[:, width : 2 * width] = acc[middle:, :].astype(BF)
        far[:, 2 * width :] = split_lanes(masks, sum_s[middle:, :]).astype(BF)


def expert_chunk(parts, experts, first, back, gate_w, up_w, down_w):
    total = sum(p.shape[0] for p in parts)
    units, width = gate_w.shape
    tile = 256
    middle = total // 2
    outs = [
        like((total, width), BF),
        like((total, units), BF),
        like((total, units), BF),
        like((total, units), BF),
        like((middle, width + LANES), F32),
        like((middle, width), BF),
        like((middle, 2 * width + LANES), BF),
    ]

    def tiled(rows):
        return pl.BlockSpec((rows, tile), lambda i: (0, i))

    return launch(
        functools.partial(expert_kernel, len(parts), experts),
        "expert_chunk",
        (first, *parts, back, gate_w, up_w, down_w),
        [scalar_spec()]
        + [whole(p.shape) for p in parts]
        + [tiled(total)]
        + [pl.BlockSpec((tile, width), lambda i: (i, 0))] * 3,
        outs,
        [whole((total, width))] + [tiled(total)] * 3 + [whole(o.shape) for o in outs[4:]],
        10 * total * width * units,
        grid=(units // tile,),
        scratch=[
            pltpu.VMEM((total, LANES), F32),
            pltpu.VMEM((total, LANES), F32),
            pltpu.VMEM((total, width), F32),
            pltpu.VMEM((total, width), F32),
        ],
    )


def merge_kernel(experts, first, near, near_out, far, *outs):
    width = near_out.shape[1]
    for cols in spans(width, TILE):
        drain(outs, (near_out[:, cols].astype(F32) + far[:, cols].astype(F32)).astype(BF), cols)
        there = slice(width + cols.start, width + cols.stop)
        drain(outs, (near[:, cols] + far[:, there].astype(F32)).astype(BF), there)
    lanes = near[:, width:] + far[:, 2 * width :].astype(F32)
    total = jnp.sum(lanes, axis=1, keepdims=True)
    value = split_lanes(lane_masks(first[0], experts), jnp.broadcast_to(total, lanes.shape))
    drain(outs, value.astype(BF), slice(2 * width, 2 * width + LANES))


def merge_rows(experts, first, near, near_out, far, parts):
    rows, cols = far.shape
    outs = [like((rows // parts, cols), BF)] * parts
    args = (first, near, near_out, far)
    return launch(
        functools.partial(merge_kernel, experts),
        "merge_rows",
        args,
        [scalar_spec()] + [whole(x.shape) for x in args[1:]],
        outs,
        [whole(o.shape) for o in outs],
        rows * cols,
    )


def shared_kernel(a, b, weight, back, back_pre, hidden, rows):
    width, units = weight.shape[0], weight.shape[1] // 2
    fill(rows, (a, b), slice(0, width))
    gate_pre = dot(rows[...], weight[:, :units])
    up_pre = dot(rows[...], weight[:, units:])
    sig = jax.nn.sigmoid(gate_pre)
    act = gate_pre * sig
    hidden[...] = (act * up_pre).astype(BF)
    grad = back[...]
    back_pre[:, :units] = (grad * up_pre * sig * (1.0 + gate_pre * (1.0 - sig))).astype(BF)
    back_pre[:, units:] = (grad * act).astype(BF)


def shared_chunk(a, b, weight, back):
    half = a.shape[0]
    units = weight.shape[1]
    args = (a, b, weight, back)
    outs = [like((2 * half, units), BF), like((2 * half, units // 2), BF)]
    return launch(
        shared_kernel,
        "shared_chunk",
        args,
        [whole(x.shape) for x in args],
        outs,
        [whole(o.shape) for o in outs],
        4 * half * weight.shape[0] * units,
        scratch=[pltpu.VMEM((2 * half, weight.shape[0]), BF)],
    )


def combine_kernel(slots, count, ids, rank_a, rank_b, *refs):
    parts = refs[:count]
    hidden, weight_out, back_pre, weight_in, near, far, rows, ranks = refs[count:]
    width = weight_in.shape[0]
    fill(rows, parts, slice(None))
    fill(ranks, (rank_a, rank_b), slice(None))
    half = near.shape[0]
    choose = choose_slots(ids, slots, ranks[...])
    for cols in spans(near.shape[1], TILE):
        value = dot(choose, rows[:, cols])
        if cols.stop <= width:
            value = value + dot_nt(hidden[...], weight_out[cols, :])
        elif cols.stop <= 2 * width:
            there = slice(cols.start - width, cols.stop - width)
            value = value + dot_nt(back_pre[...], weight_in[there, :])
        near[:, cols] = value[:half]
        far[:, cols] = value[half:].astype(BF)


def combine_rows(ids, slots, ranked, parts, hidden, weight_out, back_pre, weight_in):
    half, width = ranked[0].shape[0], weight_in.shape[0]
    total = sum(p.shape[0] for p in parts)
    cols = parts[0].shape[1]
    outs = [like((half, cols), F32), like((half, cols), BF)]
    rest = (hidden, weight_out, back_pre, weight_in)
    return launch(
        functools.partial(combine_kernel, slots, len(parts)),
        "combine_rows",
        (ids, *ranked, *parts, *rest),
        [scalar_spec()]
        + [rank_spec(half, width)] * 2
        + [whole(x.shape) for x in (*parts, *rest)],
        outs,
        [whole(o.shape) for o in outs],
        4 * half * (total * cols + (hidden.shape[1] + back_pre.shape[1]) * width),
        scratch=[pltpu.VMEM((total, cols), BF), pltpu.VMEM((2 * half, LANES), BF)],
    )


def weight_grad_kernel(count, units, pairs, *refs):
    outs = refs[-len(pairs) :]
    for out, (left, right) in zip(outs, pairs):
        total = None
        for k in range(count):
            part = dot_tn(refs[left * count + k][:, :units], refs[right * count + k][...])
            total = part if total is None else total + part
        out[...] = total


def weight_grads(lefts, rights, pairs, units):
    count = len(rights[0])
    rows, width = rights[0][0].shape
    tile = 256
    args = [x for group in (*lefts, *rights) for x in group]
    return launch(
        functools.partial(weight_grad_kernel, count, units, pairs),
        "weight_grads",
        args,
        [whole(x.shape) for group in lefts for x in group]
        + [pl.BlockSpec((rows, tile), lambda i: (0, i))] * (count * len(rights)),
        [like((units, width), F32)] * len(pairs),
        [pl.BlockSpec((units, tile), lambda i: (0, i))] * len(pairs),
        2 * len(pairs) * count * rows * width * units,
        grid=(width // tile,),
    )


def norm_kernel(count, *refs):
    parts, (gain, out) = refs[:count], refs[count:]
    row = 0
    for part in parts:
        size = part.shape[0]
        out[row : row + size, :] = rmsnorm(part[...].astype(F32), gain[...]).astype(BF)
        row += size


def norm_rows(parts, gain):
    total = sum(p.shape[0] for p in parts)
    width = parts[0].shape[1]
    gain = gain.reshape(1, width)
    return launch(
        functools.partial(norm_kernel, len(parts)),
        "norm_rows",
        (*parts, gain),
        [whole(p.shape) for p in parts] + [whole(gain.shape)],
        [like((total, width), BF)],
        [whole((total, width))],
        4 * total * width,
    )[0]


def attended_kernel(count, *refs):
    parts, (weight, attended, back, grad, rows) = refs[:count], refs[count:]
    fill(rows, parts, slice(None))
    back[...] = dot_nt(rows[...], weight[...]).astype(BF)
    for cols in spans(rows.shape[1], TILE):
        grad[:, cols] = dot_tn(attended[...], rows[:, cols]).astype(BF)


def attended_back(parts, weight, attended):
    total, cols = attended.shape
    width = weight.shape[1]
    outs = [like((total, cols), BF), like((cols, width), BF)]
    return launch(
        functools.partial(attended_kernel, len(parts)),
        "attended_back",
        (*parts, weight, attended),
        [whole(p.shape) for p in parts] + [whole(weight.shape), whole(attended.shape)],
        outs,
        [whole(o.shape) for o in outs],
        4 * total * cols * width,
        scratch=[pltpu.VMEM((total, width), BF)],
    )


def shared_grad_kernel(count, *refs):
    xs, cots = refs[: 2 * count], refs[2 * count : 4 * count]
    backs, hiddens = refs[4 * count : 5 * count], refs[5 * count : 6 * count]
    out = refs[6 * count]
    half = xs[0].shape[0]
    first = backs[0].shape[1]
    for cols, lefts, rights in (
        (slice(0, first), xs, backs),
        (slice(first, out.shape[1]), cots, hiddens),
    ):
        total = None
        for k in range(count):
            for side in range(2):
                right = rights[k][side * half : (side + 1) * half, :]
                part = dot_tn(lefts[2 * k + side][...], right)
                total = part if total is None else total + part
        out[:, cols] = total.astype(BF)


def shared_grads(xs, cots, backs, hiddens, width):
    half = xs[0].shape[0]
    tile = 256
    cols = backs[0].shape[1] + hiddens[0].shape[1]
    return launch(
        functools.partial(shared_grad_kernel, len(backs)),
        "shared_grads",
        (*xs, *cots, *backs, *hiddens),
        [pl.BlockSpec((half, tile), lambda i: (0, i))] * (len(xs) + len(cots))
        + [whole(b.shape) for b in (*backs, *hiddens)],
        [like((width, cols), BF)],
        [pl.BlockSpec((tile, cols), lambda i: (i, 0))],
        2 * len(xs) * half * width * cols,
        grid=(width // tile,),
    )[0]


def body(
    n_dp,
    n_ctx,
    tokens,
    cotangent,
    lengths,
    deal_order,
    routes,
    attn_gain,
    q_weight,
    kv_down,
    latent_gain,
    kv_up,
    out_weight,
    ffn_gain,
    router,
    shared_gate,
    shared_up,
    shared_down,
    expert_gate,
    expert_up,
    expert_down,
):
    rows, width = tokens.shape
    half = rows // 2
    top = routes.shape[1]
    experts = router.shape[1]
    blocks = n_dp * n_ctx
    band = width // blocks
    slots = 4 * rows * top // (3 * experts) // 2
    z = lax.axis_index("dp")
    c = lax.axis_index("ctx")
    t = lax.axis_index("tp")
    expert_id = z * n_ctx + c
    width_qk = NOPE + ROPE
    width_kv = NOPE + VDIM
    scale_factor = width_qk ** (-0.5)
    heads = q_weight.shape[1] // width_qk // n_ctx
    pack = rows * n_ctx

    def across(x, j):
        return lax.ppermute(x, "ctx", [(i, i ^ j) for i in range(n_ctx)])

    def swap(x):
        return lax.ppermute(x, "tp", [(0, 1), (1, 0)])

    def hop(x):
        return lax.ppermute(x, "dp", [(i, (i + 1) % n_dp) for i in range(n_dp)])

    def own_half(x):
        return lax.dynamic_slice_in_dim(x, t * half, half)

    def both_halves(x):
        other = swap(x)
        first = t == 0
        return jnp.concatenate([jnp.where(first, x, other), jnp.where(first, other, x)], axis=0)

    def gather_parts(x):
        near = [x] + [across(x, j) for j in range(1, n_ctx)]
        return near + [swap(p) for p in near]

    def scatter_pack(near, far):
        near = (near + swap(far).astype(F32)).reshape(n_ctx, half, near.shape[1])
        return near[0], [across(near[j].astype(BF), j) for j in range(1, n_ctx)]

    def gathered(own, parts, *marks):
        for part in after(parts, *marks):
            own = own + part.astype(F32)
        return own

    def after(values, *marks):
        return lax.optimization_barrier((values, *marks))[0]

    q_cols, out_rows = heads * width_qk, heads * VDIM
    up_cols = heads * width_kv
    up_rows = kv_up.shape[0]
    folds = up_cols // LANES
    lead_cols = q_cols + LANES
    nope_cols = heads * NOPE

    def plane_order(near):
        bit = 1
        while bit < n_ctx:
            shape = near.shape
            pairs = near.reshape((n_ctx // (2 * bit), 2, bit) + shape[1:])
            near = jnp.where((c & bit) > 0, pairs[:, ::-1], pairs).reshape(shape)
            bit *= 2
        return near

    def ring_of(x):
        ring = [x]
        for _ in range(n_dp - 1):
            ring.append(hop(ring[-1]))
        return ring

    def collect(ring, take, block):
        total = None
        for k, x in enumerate(ring):
            part = take(x)
            if total is None:
                total = jnp.zeros((n_dp * block,) + part.shape[1:], part.dtype)
            total = lax.dynamic_update_slice_in_dim(total, part, ((z - k) % n_dp) * block, 0)
        return total

    small = jnp.concatenate([attn_gain, ffn_gain, latent_gain, router.reshape(band * experts)])
    small_rows = -(-small.shape[0] // lead_cols)
    small = jnp.pad(small, (0, small_rows * lead_cols - small.shape[0]))
    small = small.reshape(small_rows, lead_cols)

    def lead_piece(j):
        q = lax.dynamic_slice_in_dim(q_weight, (c ^ j) * q_cols, q_cols, 1)
        q = q.reshape(band, heads, width_qk)
        q = jnp.concatenate(
            [q[..., :NOPE].reshape(band, nope_cols), q[..., NOPE:].reshape(band, -1)], axis=1
        )
        up = lax.dynamic_slice_in_dim(kv_up, (c ^ j) * up_cols, up_cols, 1)
        up = up.reshape(up_rows, folds, LANES).transpose(1, 0, 2).reshape(folds * up_rows, LANES)
        return jnp.concatenate([jnp.concatenate([q, up], axis=1), small], axis=0)

    def out_piece(j):
        return lax.dynamic_slice_in_dim(out_weight, (c ^ j) * out_rows, out_rows, 0)

    lead = [lead_piece(0)] + [across(lead_piece(j), j) for j in range(1, n_ctx)]
    lead = plane_order(jnp.stack(lead))
    own_tokens_low = own_half(tokens)
    token_parts = gather_parts(after(own_tokens_low, lead))
    lead_ring = ring_of(lead)
    q_mine = collect(lead_ring, lambda x: x[:, :band, :q_cols].reshape(-1, q_cols), n_ctx * band)
    up_mine = collect(
        lead_ring,
        lambda x: x[:, :band, q_cols:]
        .reshape(n_ctx, folds, up_rows, LANES)
        .transpose(0, 2, 1, 3)
        .reshape(n_ctx * up_rows, up_cols),
        n_ctx * up_rows,
    )
    small_all = collect(lead_ring, lambda x: x[:, band:], n_ctx).reshape(blocks, -1)
    attn_gain_all = small_all[:, :band].reshape(width).astype(F32)
    ffn_gain_all = small_all[:, band : 2 * band].reshape(width).astype(F32)
    latent_cols = latent_gain.shape[0]
    latent_gain_all = (
        small_all[:, 2 * band : 2 * band + latent_cols].reshape(KV_RANK).astype(F32)
    )
    router_all = small_all[:, 2 * band + latent_cols : 2 * band + latent_cols + band * experts]
    router_all = router_all.reshape(width, experts)

    down_half = lax.dynamic_slice_in_dim(kv_down, t * (band // 2), band // 2)
    down_all = lax.all_gather(down_half, ("dp", "ctx", "tp"), axis=0, tiled=True)

    out_near = plane_order(
        jnp.stack([out_piece(0)] + [across(after(out_piece(j), q_mine), j) for j in range(1, n_ctx)])
    )
    out_mine = (
        lax.all_gather(out_near, "dp", axis=0, tiled=True)
        .transpose(1, 0, 2)
        .reshape(out_rows, width)
    )

    groups = -(-shared_gate.shape[1] // (LANES * n_dp))
    hidden_units = groups * LANES
    all_units = hidden_units * n_dp

    def widen(x, cols):
        return jnp.pad(x, ((0, 0), (0, cols - x.shape[1])))

    def unit_pieces(w):
        return widen(w, all_units).reshape(band, n_dp, hidden_units).transpose(1, 0, 2)

    shared_send = jnp.concatenate(
        [unit_pieces(w) for w in (shared_gate, shared_up, shared_down.T)], axis=2
    )
    units = expert_gate.shape[2]
    padded_units = -(-units // 256) * 256
    gate_w, up_w, expert_out = (
        after(jnp.pad(w, ((0, padded_units - units), (0, 0))), lead_ring[1])
        for w in (expert_gate[0].T, expert_up[0].T, expert_down[0])
    )

    order_index = (c ^ jnp.arange(n_ctx))[None, :] * 2 + (t ^ jnp.arange(2))[:, None]
    order_row = deal_order[0].reshape(n_ctx * 2, half)[order_index.reshape(-1)].reshape(pack)
    docs, pos = places(lengths[0], order_row)
    cos_table, sin_table = rope_tables(pos)
    own_cot = own_half(cotangent)
    expert_row = jnp.arange(experts, dtype=jnp.int32)
    hot = jnp.sum((routes[:, :, None] == expert_row[None, None, :]).astype(BF), axis=1)
    row_index = jnp.arange(rows)
    earlier = (row_index[:, None] >= row_index[None, :]).astype(BF)
    rank = dot(earlier, hot) * hot.astype(F32)

    cot_extended = jnp.concatenate(
        [own_cot, own_half(rank).astype(BF), jnp.zeros((half, LANES - experts), BF)], axis=1
    )
    ids = jnp.concatenate(
        [
            (z * n_ctx + (c ^ jnp.arange(n_ctx, dtype=jnp.int32))).astype(jnp.int32),
            (t * slots + 1).astype(jnp.int32).reshape(1),
        ]
    )
    apart = n_ctx if slots % 16 == 0 else 1

    def exchange(parts):
        if apart == 1:
            parts = [parts[0][j * slots : (j + 1) * slots] for j in range(n_ctx)]
        parts = [parts[0]] + [across(parts[j], j) for j in range(1, n_ctx)]
        return parts if apart > 1 else [jnp.concatenate(parts, axis=0)]

    def both_cores(parts):
        return parts + [swap(p) for p in parts]

    cot_pairs, cot_parts = [], []

    def cot_step(x):
        pair = (x, swap(x))
        picked = pick_rows(ids, slots, pair, *pair, width, width, apart)
        cot_pairs.append(pair)
        cot_parts.append(exchange(picked))

    cot_step(cot_extended)
    normed_low = norm_rows(after(token_parts, cot_parts[0]), attn_gain_all)
    query_pre = dot(normed_low, q_mine)
    query_turned = rotate(
        query_pre[:, nope_cols:].reshape(pack, heads, ROPE),
        cos_table[:, None],
        sin_table[:, None],
    )
    latent_pre = dot(normed_low, down_all)
    latent_low = rmsnorm(latent_pre[:, :KV_RANK], latent_gain_all).astype(BF)
    rope_low = rotate(latent_pre[:, KV_RANK:], cos_table, sin_table).astype(BF)
    if n_dp > 1:
        cot_step(after(hop(after(cot_extended, q_mine)), latent_low))
    expanded = dot(latent_low, up_mine).astype(BF)
    allowed = (docs[:, None] == docs[None, :]) & (pos[None, :] <= pos[:, None])
    queries, keys, values, log_totals, attended = [], [], [], [], []

    def scores_of(h):
        return jnp.where(allowed, dot_nt(queries[h], keys[h]) * scale_factor, NEGATIVE)

    for h in range(heads):
        queries.append(
            jnp.concatenate(
                [query_pre[:, h * NOPE : (h + 1) * NOPE], query_turned[:, h]], axis=1
            ).astype(BF)
        )
        base = h * width_kv
        keys.append(jnp.concatenate([expanded[:, base : base + NOPE], rope_low], axis=1))
        values.append(expanded[:, base + NOPE : base + width_kv])
        scores = scores_of(h)
        highest = jnp.max(scores, axis=-1, keepdims=True)
        exponentials = jnp.exp(scores - highest)
        totals = jnp.sum(exponentials, axis=-1, keepdims=True)
        log_totals.append(highest + jnp.log(totals))
        attended.append(dot((exponentials / totals).astype(BF), values[h]).astype(BF))
    first_attended = attended[0]
    attended = jnp.concatenate(attended, axis=1)
    own_tokens = own_tokens_low.astype(F32)
    middle = pack // 2
    attended = after(attended, cot_parts[-1])
    attended_far = dot(attended[middle:], out_mine).astype(BF)
    own_attended, attended_parts = scatter_pack(dot(attended[:middle], out_mine), attended_far)

    shared_part = lax.all_to_all(
        after(shared_send, cot_pairs[-1][0]), "dp", split_axis=0, concat_axis=0, tiled=True
    )
    shared_all = (
        lax.all_gather(after(shared_part, own_attended), "ctx", axis=0, tiled=False)
        .transpose(1, 0, 2, 3)
        .reshape(width, 3 * hidden_units)
    )
    shared_in = shared_all[:, : 2 * hidden_units]
    shared_out_t = shared_all[:, 2 * hidden_units :]

    for k in range(max(2, 1), n_dp):
        cot_step(after(hop(cot_pairs[k - 1][0]), own_attended))
    back_hidden, cot_rows = [], []
    for k in range(n_dp):
        back, rows_in = cot_product(both_cores(after(cot_parts[k], own_attended)), expert_out)
        back_hidden.append(back)
        cot_rows.append(rows_in)
    hidden_one = gathered(own_tokens + own_attended, attended_parts, back_hidden[:2])

    ffn_normed, ffn_norm_back = jax.vjp(rmsnorm, hidden_one, ffn_gain_all)
    ffn_low = ffn_normed.astype(BF)
    router_probs = jax.nn.softmax(dot(ffn_low, router_all), axis=-1)
    probs_high, probs_low = two_parts(router_probs)
    spare = jnp.zeros((half, LANES - 2 * experts), BF)
    ffn_ring = ring_of(jnp.concatenate([ffn_low, probs_high, probs_low, spare], axis=1))
    first = jnp.full((1,), expert_id, jnp.int32)

    back_shared = cot_shared(after(cot_pairs, ffn_ring[0]), shared_out_t)
    mark = [back_hidden[-1]]

    def in_turn(run, args, *rest):
        result = run(*after(args, mark[0]), *rest)
        mark[0] = result[0] if isinstance(result, (list, tuple)) else result
        return result

    pairs, x_near, x_in, shared_hidden, back_shared_pre = [], [], [], [], []
    x_rows, back_gates, back_ups, gated, nears, fars, returned = [], [], [], [], [], [], []
    combined = [None] * n_dp

    def pick_chunk(k):
        pairs.append((ffn_ring[k], swap(ffn_ring[k])))
        picked = in_turn(
            lambda *pair: pick_rows(ids, slots, cot_pairs[k], *pair, width, width + LANES, apart),
            pairs[k],
        )
        x_near.append(exchange(picked))

    def share_chunk(k):
        back_pre, hidden = in_turn(
            lambda *pair: shared_chunk(*pair, shared_in, back_shared[k]), pairs[k]
        )
        back_shared_pre.append(back_pre)
        shared_hidden.append(hidden)

    def run_expert(k):
        x, back_gate, back_up, gated_hidden, near, near_out, far = in_turn(
            lambda *parts: expert_chunk(
                list(parts), experts, first, back_hidden[k], gate_w, up_w, expert_out
            ),
            x_in[k],
        )
        x_rows.append(x)
        back_gates.append(back_gate)
        back_ups.append(back_up)
        gated.append(gated_hidden)
        nears.append((near, near_out))
        fars.append(swap(far))

    def merge_chunk(k):
        merged = in_turn(
            lambda *parts: merge_rows(experts, first, *parts, apart), (*nears[k], fars[k])
        )
        returned.append(exchange(merged))

    def combine_chunk(k):
        combined[k] = in_turn(
            lambda *parts: combine_rows(
                ids,
                slots,
                cot_pairs[k],
                parts,
                shared_hidden[k],
                shared_out_t,
                back_shared_pre[k],
                shared_in,
            ),
            returned[k],
        )

    pick_chunk(0)
    if n_dp > 1:
        pick_chunk(1)
    for k in range(n_dp):
        ahead = ffn_ring[min(k + 3, n_dp - 1)]
        x_in.append(both_cores(after(x_near[k], mark[0], ahead)))
        if k == 0:
            share_chunk(0)
        run_expert(k)
        if k + 1 < n_dp:
            share_chunk(k + 1)
        elif k:
            combine_chunk(k - 1)
        merge_chunk(k)
        if k + 2 < n_dp:
            pick_chunk(k + 2)
        if 0 < k < n_dp - 1:
            combine_chunk(k - 1)
    grad_egate, grad_eup = in_turn(
        lambda *gates: weight_grads([gates, back_ups], [x_rows], ((0, 2), (1, 2)), units),
        back_gates,
    )
    combine_chunk(n_dp - 1)
    x_pairs = [x for pair in pairs for x in pair]
    cot_flat = [x for pair in cot_pairs for x in pair]
    grad_shared = in_turn(
        lambda *xs: shared_grads(xs, cot_flat, back_shared_pre, shared_hidden, width), x_pairs
    )
    grad_shared = grad_shared.reshape(n_dp, n_ctx, band, 3 * hidden_units)
    grad_shared = grad_shared.transpose(1, 0, 2, 3).reshape(width, 3 * hidden_units)
    shared_sums = grad_shared
    grad_shared = lax.psum_scatter(grad_shared, "ctx", scatter_dimension=0, tiled=True)
    total = None
    for step in range(1, n_dp + 1):
        near, far = combined[step % n_dp]
        near = near + swap(far).astype(F32)
        if total is not None:
            total = hop(total.astype(BF))
            near = near + (after(total, shared_sums) if step == n_dp else total).astype(F32)
        total = near
    output_sum, back_ffn = total[:, :width], total[:, width:]
    back_probs = (
        back_ffn[:, width : width + experts] + back_ffn[:, width + experts : width + 2 * experts]
    )
    back_logits = router_probs * (
        back_probs - jnp.sum(router_probs * back_probs, axis=-1, keepdims=True)
    )
    back_ffn_normed = back_ffn[:, :width] + jnp.dot(
        back_logits, router_all.astype(F32).T, precision=PRECISE
    )
    grad_router = jnp.dot(back_logits.T, ffn_low.astype(F32), precision=PRECISE)
    back_hidden_one, grad_ffn_gain = ffn_norm_back(back_ffn_normed)
    back_hidden_one = back_hidden_one + own_cot.astype(F32)

    back_parts = gather_parts(back_hidden_one.astype(BF))
    mark[0] = back_hidden_one
    (grad_edown,) = in_turn(
        lambda *gates: weight_grads([gates], [cot_rows], ((0, 1),), units), gated
    )
    back_parts = after(back_parts, grad_edown)
    output = both_halves((hidden_one + output_sum).astype(BF))

    back_attended, grad_out_t = attended_back(back_parts, out_mine, attended)
    grad_shared = lax.all_to_all(
        after(grad_shared, back_parts).reshape(n_dp, band, 3 * hidden_units),
        "dp",
        split_axis=0,
        concat_axis=0,
        tiled=True,
    ).astype(F32)
    back_nope, back_turned, back_expanded, back_rope = [], [], [], None
    for h in range(heads):
        back_head = back_attended[:, h * VDIM : (h + 1) * VDIM]
        probabilities = jnp.exp(scores_of(h) - log_totals[h])
        back_prob = dot_nt(back_head, values[h])
        inner_sum = jnp.sum(probabilities * back_prob, axis=-1, keepdims=True)
        back_raw = (probabilities * (back_prob - inner_sum) * scale_factor).astype(BF)
        back_query = dot(back_raw, keys[h])
        back_key = dot_tn(back_raw, queries[h])
        back_nope.append(back_query[:, :NOPE].astype(BF))
        back_turned.append(unrotate(back_query[:, NOPE:], cos_table, sin_table).astype(BF))
        back_expanded.append(back_key[:, :NOPE].astype(BF))
        back_expanded.append(dot_tn(probabilities.astype(BF), back_head).astype(BF))
        turned = back_key[:, NOPE:]
        back_rope = turned if back_rope is None else back_rope + turned
    back_nope = after(back_nope, grad_shared)
    back_query_pre = jnp.concatenate(back_nope + back_turned, axis=1)
    back_expanded = jnp.concatenate(back_expanded, axis=1)
    back_latent = jnp.concatenate(
        [dot_nt(back_expanded, up_mine), back_rope, jnp.zeros((pack, ROPE), F32)], axis=1
    )
    own_latent_back, latent_parts = scatter_pack(
        back_latent[:middle], back_latent[middle:].astype(BF)
    )
    back_far = dot_nt(back_query_pre[middle:], q_mine).astype(BF)
    own_back, back_sum_parts = scatter_pack(dot_nt(back_query_pre[:middle], q_mine), back_far)
    grad_heads = jnp.concatenate(
        [
            dot_tn(normed_low, back_query_pre),
            grad_out_t.T,
            dot_tn(latent_low, back_expanded)
            .reshape(blocks, up_rows, folds, LANES)
            .transpose(0, 2, 1, 3)
            .reshape(width, LANES),
        ],
        axis=1,
    ).astype(BF)
    back_latent = gathered(own_latent_back, latent_parts, grad_heads)
    own_latent = latent_pre[:half, :KV_RANK]
    back_latent_pre, grad_latent_gain = jax.vjp(rmsnorm, own_latent, latent_gain_all)[1](
        back_latent[:, :KV_RANK]
    )
    back_down = jnp.concatenate(
        [
            back_latent_pre,
            unrotate(
                back_latent[:, KV_RANK : KV_RANK + ROPE], cos_table[:half], sin_table[:half]
            ),
        ],
        axis=1,
    ).astype(BF)
    back_down_parts = gather_parts(back_down)
    back_sum = gathered(own_back, back_sum_parts)
    back_normed = back_sum + dot_nt(back_down, down_all)
    back_inputs, grad_attn_gain = jax.vjp(rmsnorm, own_tokens, attn_gain_all)[1](back_normed)
    input_grad = both_halves(back_hidden_one + back_inputs)

    grad_sgate, grad_sup, grad_sdown = (
        grad_shared[:, :, i * hidden_units : (i + 1) * hidden_units]
        .transpose(1, 0, 2)
        .reshape(band, all_units)[:, : shared_gate.shape[1]]
        for i in range(3)
    )

    grad_heads = lax.psum_scatter(grad_heads, "dp", scatter_dimension=0, tiled=True)
    grad_heads = lax.all_to_all(
        grad_heads.reshape(n_ctx, band, -1), "ctx", split_axis=0, concat_axis=0, tiled=True
    ).astype(F32)
    grad_q = jnp.concatenate(
        [
            grad_heads[:, :, :nope_cols].reshape(n_ctx, band, heads, NOPE),
            grad_heads[:, :, nope_cols:q_cols].reshape(n_ctx, band, heads, ROPE),
        ],
        axis=3,
    )
    grad_q = grad_q.transpose(1, 0, 2, 3).reshape(band, n_ctx * q_cols)
    grad_out = (
        grad_heads[:, :, q_cols : q_cols + out_rows]
        .transpose(0, 2, 1)
        .reshape(n_ctx * out_rows, band)
    )
    grad_up = (
        grad_heads[:, :, q_cols + out_rows :]
        .reshape(n_ctx, folds, up_rows, LANES)
        .transpose(2, 0, 1, 3)
        .reshape(up_rows, n_ctx * up_cols)
    )
    back_down_pack = jnp.concatenate(back_down_parts, axis=0)
    normed_band = jnp.concatenate(
        [
            lax.dynamic_slice_in_dim(normed_low, (i * n_ctx + c) * band, band, axis=1)
            for i in range(n_dp)
        ],
        axis=1,
    )
    down_sums = dot_tn(normed_band, back_down_pack).reshape(n_dp, band, -1)
    grad_down = lax.dynamic_index_in_dim(down_sums, z, 0, keepdims=False)
    for i in range(1, n_dp):
        sent = lax.dynamic_index_in_dim(down_sums, (z + i) % n_dp, 0, keepdims=False)
        sent = lax.ppermute(sent.astype(BF), "dp", [(a, (a + i) % n_dp) for a in range(n_dp)])
        grad_down = grad_down + sent.astype(F32)
    late = jnp.concatenate(
        [
            grad_router.reshape(experts, blocks, band).transpose(1, 0, 2),
            grad_ffn_gain.reshape(blocks, 1, band),
            grad_attn_gain.reshape(blocks, 1, band),
            widen(grad_latent_gain.reshape(blocks, latent_cols), band)[:, None],
        ],
        axis=1,
    )
    late = jnp.sum(
        lax.all_to_all(late + swap(late), GRID, split_axis=0, concat_axis=0, tiled=True), axis=0
    )
    return (
        output,
        input_grad,
        late[experts + 1],
        grad_q,
        grad_down,
        late[experts + 2, :latent_cols],
        grad_up,
        grad_out,
        late[experts],
        late[:experts].T,
        grad_sgate,
        grad_sup,
        grad_sdown.T,
        grad_egate.T[None],
        grad_eup.T[None],
        grad_edown[None],
    )


def solution(mesh):
    n_dp, n_ctx = mesh.shape["dp"], mesh.shape["ctx"]
    ins = (
        P(GRID, None),
        P(GRID, None),
        P("dp", None),
        P("dp", None),
        P(GRID, None),
        P(GRID),
        P(GRID, "tp"),
        P(GRID, None),
        P(GRID),
        P(GRID, "tp"),
        P("tp", GRID),
        P(GRID),
        P(GRID, None),
        P(GRID, "tp"),
        P(GRID, "tp"),
        P("tp", GRID),
        P(GRID, None, "tp"),
        P(GRID, None, "tp"),
        P(GRID, "tp", None),
    )
    outs = (
        P(GRID, None),
        P(GRID, None),
        P(GRID),
        P(GRID, "tp"),
        P(GRID, None),
        P(GRID),
        P(GRID, "tp"),
        P("tp", GRID),
        P(GRID),
        P(GRID, None),
        P(GRID, "tp"),
        P(GRID, "tp"),
        P("tp", GRID),
        P(GRID, None, "tp"),
        P(GRID, None, "tp"),
        P(GRID, "tp", None),
    )
    return jax.shard_map(
        functools.partial(body, n_dp, n_ctx),
        mesh=mesh,
        in_specs=ins,
        out_specs=outs,
        check_vma=False,
    )
```

```python
import functools
import math

import jax
import jax.numpy as jnp
from jax import lax
from jax.experimental import pallas as pl
from jax.experimental.pallas import tpu as pltpu
from jax.sharding import PartitionSpec as P

NOPE = 128
ROPE = 64
VDIM = 128
KV_RANK = 512
LANES = 128

EPSILON = 1e-06
NEGATIVE = -1e30
PRECISE = lax.Precision.HIGHEST
BF = jnp.bfloat16
F32 = jnp.float32
GRID = ("dp", "ctx")


def rmsnorm(values, gain_vec):
    return (
        values * lax.rsqrt(jnp.mean(values * values, axis=-1, keepdims=True) + EPSILON) * gain_vec
    )


def rope_tables(position):
    frequency = jnp.exp(
        jnp.arange(ROPE // 2, dtype=F32) * (-2.0 * math.log(10000.0) / ROPE)
    )
    angle_table = position.astype(F32)[:, None] * frequency[None, :]
    return (jnp.cos(angle_table), jnp.sin(angle_table))


def rotate(values, cos_table, sin_table):
    half_size = values.shape[-1] // 2
    first_half = values[..., :half_size]
    second_half = values[..., half_size:]
    return jnp.concatenate(
        [
            first_half * cos_table - second_half * sin_table,
            first_half * sin_table + second_half * cos_table,
        ],
        axis=-1,
    )


def unrotate(values, cos_table, sin_table):
    return rotate(values, cos_table, -sin_table)


def places(lengths_row, order_row):
    doc_ends = jnp.cumsum(lengths_row)
    starts = doc_ends - lengths_row
    doc_ids = jnp.sum((order_row[:, None] >= doc_ends[None, :]).astype(jnp.int32), axis=1)
    matched = doc_ids[:, None] == jnp.arange(lengths_row.shape[0], dtype=jnp.int32)[None, :]
    doc_start = jnp.sum(jnp.where(matched, starts[None, :], 0), axis=1)
    return (doc_ids, order_row - doc_start)


def dot(left, right):
    return jnp.dot(left, right, preferred_element_type=F32)


def dot_nt(left, right):
    return lax.dot_general(left, right, (((1,), (1,)), ((), ())), preferred_element_type=F32)


def dot_tn(left, right):
    return lax.dot_general(left, right, (((0,), (0,)), ((), ())), preferred_element_type=F32)


def two_parts(values):
    high = lax.reduce_precision(values, 8, 7)
    return high.astype(BF), (values - high).astype(BF)


TILE = 512
EAGER = 4


def whole(shape):
    return pl.BlockSpec(shape, lambda *_: (0,) * len(shape))


def scalar_spec():
    return pl.BlockSpec(memory_space=pltpu.SMEM)


def like(shape, dtype):
    return jax.ShapeDtypeStruct(shape, dtype)


def launch(kernel, name, args, in_specs, outs, out_specs, flops, grid=(1,), scratch=()):
    moved = sum(math.prod(a.shape) * a.dtype.itemsize for a in (*args, *outs))
    return pl.pallas_call(
        kernel,
        grid=grid,
        in_specs=in_specs,
        out_specs=out_specs,
        out_shape=outs,
        scratch_shapes=scratch,
        name=name,
        cost_estimate=pl.CostEstimate(
            flops=flops // EAGER, bytes_accessed=moved // EAGER, transcendentals=0
        ),
    )(*args)


def spans(total, step):
    return [slice(lo, min(lo + step, total)) for lo in range(0, total, step)]


def fill(ref, parts, cols):
    row = 0
    for part in parts:
        size = part.shape[-2]
        value = part[..., cols]
        ref[row : row + size, :] = value.reshape(size, value.shape[-1])
        row += size


def drain(outs, value, cols):
    row = 0
    for out in outs:
        size = out.shape[0]
        out[:, cols] = value[row : row + size]
        row += size


def slot_places(ids, slots, ranks):
    plane = ids.shape[0] - 1
    lane = lax.broadcasted_iota(jnp.int32, (8, LANES), 1)
    sub = lax.broadcasted_iota(jnp.int32, (8, LANES), 0)
    found = jnp.zeros((8, LANES), F32)
    for j in range(plane):
        found = jnp.where((sub == j) & (lane == ids[j]), 1.0, found)
    return found.astype(BF), ids[plane].astype(F32), plane


def within(number, first, slots, base):
    place = number - first
    return jnp.where((place >= 0) & (place < slots), place + base, -1.0)


def choose_rows(ids, slots, ranks, g, group):
    found, first, plane = slot_places(ids, slots, ranks)
    numbers = dot_nt(found, ranks)
    total, rows = plane * group * slots, ranks.shape[0]
    place = lax.broadcasted_iota(jnp.int32, (total, rows), 0).astype(F32)
    chosen = jnp.zeros((total, rows), F32)
    for j in range(plane):
        there = within(numbers[j : j + 1, :], first, slots, (j * group + g) * slots)
        chosen = jnp.where(place == there, 1.0, chosen)
    return chosen.astype(BF)


def choose_slots(ids, slots, ranks, g, group):
    found, first, plane = slot_places(ids, slots, ranks)
    numbers = dot_nt(ranks, found)
    total, rows = plane * group * slots, ranks.shape[0]
    place = lax.broadcasted_iota(jnp.int32, (rows, total), 1).astype(F32)
    chosen = jnp.zeros((rows, total), F32)
    for j in range(plane):
        there = within(numbers[:, j : j + 1], first, slots, (j * group + g) * slots)
        chosen = jnp.where(place == there, 1.0, chosen)
    return chosen.astype(BF)


def pick_kernel(slots, group, ids, *refs):
    ranked, pairs = refs[: 2 * group], refs[2 * group : 4 * group]
    outs, (ranks, rows) = refs[4 * group : -2], refs[-2:]
    cols = rows.shape[1]
    half = ranked[0].shape[0]
    chosen = []
    for g in range(group):
        fill(ranks, ranked[2 * g : 2 * g + 2], slice(None))
        chosen.append(choose_rows(ids, slots, ranks[...], g, group))
        for side in range(2):
            row = (2 * g + side) * half
            rows[row : row + half, :] = pairs[2 * g + side][:, :cols]
    for span in spans(cols, TILE):
        value = None
        for g in range(group):
            part = dot(chosen[g], rows[2 * g * half : 2 * (g + 1) * half, span])
            value = part if value is None else value + part
        drain(outs, value.astype(BF), span)


def rank_spec(half, width):
    return pl.BlockSpec((half, LANES), lambda *_: (0, width // LANES))


def pick_rows(ids, slots, ranked, blocks, width, cols, parts):
    half = blocks[0].shape[0]
    group = len(blocks) // 2
    total = (ids.shape[0] - 1) * slots * group
    outs = [like((total // parts, cols), BF)] * parts
    return launch(
        functools.partial(pick_kernel, slots, group),
        "pick_rows",
        (ids, *ranked, *blocks),
        [scalar_spec()]
        + [rank_spec(half, width)] * (2 * group)
        + [whole((half, cols))] * (2 * group),
        outs,
        [whole(o.shape) for o in outs],
        4 * group * total * half * cols,
        scratch=[
            pltpu.VMEM((2 * half, LANES), BF),
            pltpu.VMEM((2 * group * half, cols), BF),
        ],
    )


def cot_kernel(count, *refs):
    parts, (weight, back, rows) = refs[:count], refs[count:]
    fill(rows, parts, slice(None))
    for cols in spans(weight.shape[0], 256):
        back[:, cols] = dot_nt(rows[...], weight[cols, :])


def cot_product(parts, weight):
    total = sum(p.shape[0] for p in parts)
    units, width = weight.shape
    outs = [like((total, units), F32), like((total, width), BF)]
    return launch(
        functools.partial(cot_kernel, len(parts)),
        "cot_product",
        (*parts, weight),
        [whole(p.shape) for p in parts] + [whole(weight.shape)],
        outs,
        [whole(o.shape) for o in outs],
        2 * total * units * width,
    )


def cot_shared_kernel(count, *refs):
    parts, weight, outs = refs[:count], refs[count], refs[count + 1 :]
    half = parts[0].shape[0]
    for k, part in enumerate(parts):
        row = (k % 2) * half
        outs[k // 2][row : row + half, :] = dot(part[...], weight[...])


def cot_shared(pairs, weight):
    parts = [x for pair in pairs for x in pair]
    half = parts[0].shape[0]
    width, units = weight.shape
    outs = [like((2 * half, units), F32)] * len(pairs)
    return launch(
        functools.partial(cot_shared_kernel, len(parts)),
        "cot_shared",
        (*parts, weight),
        [whole((half, width))] * len(parts) + [whole(weight.shape)],
        outs,
        [whole(o.shape) for o in outs],
        2 * len(parts) * half * units * width,
    )


def lane_masks(first, experts):
    lane = lax.broadcasted_iota(jnp.int32, (1, LANES), 1)
    return lane == first, lane == first + experts


def split_lanes(masks, value):
    high = value.astype(BF).astype(F32)
    return jnp.where(masks[0], high, jnp.where(masks[1], value - high, 0.0))


def expert_kernel(count, experts, tiles, first, *refs):
    parts = refs[:count]
    back, gate_w, up_w, gate_c, up_c, down_c, x, back_gate, back_up, gated = refs[
        count : count + 10
    ]
    near, near_out, lanes_out, far, gate_s, sum_s = refs[count + 10 :]
    step = pl.program_id(0)
    width = gate_w.shape[1]
    middle = near.shape[0]
    tile = gate_w.shape[0]
    masks = lane_masks(first[0], experts)

    @pl.when(step == 0)
    def _():
        fill(x, parts, slice(0, width))
        row = 0
        for part in parts:
            size = part.shape[0]
            lanes = part[:, width:].astype(F32)
            gate = jnp.sum(jnp.where(masks[0] | masks[1], lanes, 0.0), axis=1, keepdims=True)
            gate_s[row : row + size, :] = jnp.broadcast_to(gate, (size, LANES))
            row += size
        sum_s[...] = jnp.zeros_like(sum_s)

    @pl.when(step < tiles)
    def _():
        there = pl.ds(pl.multiple_of(step * tile, tile), tile)
        for rows in spans(x.shape[0], 2 * TILE):
            gate_pre = dot_nt(x[rows, :], gate_w[...])
            up_pre = dot_nt(x[rows, :], up_w[...])
            gate = gate_s[rows, :1]
            back_hidden = back[rows, :]
            sig = jax.nn.sigmoid(gate_pre)
            act = gate_pre * sig
            hidden = act * up_pre
            gated[rows, there] = (gate * hidden).astype(BF)
            total = jnp.sum(hidden * back_hidden, axis=1, keepdims=True)
            sum_s[rows, :] += jnp.broadcast_to(total, (total.shape[0], LANES))
            scaled = gate * back_hidden
            back_up[rows, there] = (scaled * act).astype(BF)
            back_gate[rows, there] = (
                scaled * up_pre * sig * (1.0 + gate_pre * (1.0 - sig))
            ).astype(BF)

    @pl.when(step >= tiles)
    def _():
        cols = gate_c.shape[1]
        start = pl.multiple_of((step - tiles) * cols, cols)
        value = dot(back_gate[...], gate_c[...]) + dot(back_up[...], up_c[...])
        near[...] = value[:middle]
        far[:, pl.ds(width + start, cols)] = value[middle:].astype(BF)
        value = dot(gated[...], down_c[...])
        near_out[...] = value[:middle].astype(BF)
        far[:, pl.ds(start, cols)] = value[middle:].astype(BF)

    @pl.when(step == tiles)
    def _():
        lanes_out[...] = jnp.where(masks[0], sum_s[:middle, :], 0.0)
        far[:, 2 * width :] = split_lanes(masks, sum_s[middle:, :]).astype(BF)


def expert_chunk(parts, experts, first, back, gate_w, up_w, down_w):
    total = sum(p.shape[0] for p in parts)
    units, width = gate_w.shape
    tile, cols = 256, 256
    tiles, steps = units // tile, width // cols
    middle = total // 2
    outs = [
        like((total, width), BF),
        like((total, units), BF),
        like((total, units), BF),
        like((total, units), BF),
        like((middle, width), F32),
        like((middle, width), BF),
        like((middle, LANES), F32),
        like((middle, 2 * width + LANES), BF),
    ]

    def one(i):
        return jnp.minimum(i, tiles - 1)

    def two(i):
        return jnp.maximum(i - tiles, 0)

    return launch(
        functools.partial(expert_kernel, len(parts), experts, tiles),
        "expert_chunk",
        (first, *parts, back, gate_w, up_w, gate_w, up_w, down_w),
        [scalar_spec()]
        + [whole(p.shape) for p in parts]
        + [pl.BlockSpec((total, tile), lambda i: (0, one(i)))]
        + [pl.BlockSpec((tile, width), lambda i: (one(i), 0))] * 2
        + [pl.BlockSpec((units, cols), lambda i: (0, two(i)))] * 3,
        outs,
        [whole(o.shape) for o in outs[:4]]
        + [pl.BlockSpec((middle, cols), lambda i: (0, two(i)))] * 2
        + [whole(o.shape) for o in outs[6:]],
        10 * total * width * units,
        grid=(tiles + steps,),
        scratch=[pltpu.VMEM((total, LANES), F32), pltpu.VMEM((total, LANES), F32)],
    )


def merge_kernel(experts, first, near, near_out, lanes, far, *outs):
    width = near_out.shape[1]
    for cols in spans(width, TILE):
        drain(outs, (near_out[:, cols].astype(F32) + far[:, cols].astype(F32)).astype(BF), cols)
        there = slice(width + cols.start, width + cols.stop)
        drain(outs, (near[:, cols] + far[:, there].astype(F32)).astype(BF), there)
    total = jnp.sum(lanes[...] + far[:, 2 * width :].astype(F32), axis=1, keepdims=True)
    value = split_lanes(lane_masks(first[0], experts), jnp.broadcast_to(total, lanes.shape))
    drain(outs, value.astype(BF), slice(2 * width, 2 * width + LANES))


def merge_rows(experts, pieces, first, near, near_out, lanes, far):
    args = (first, near, near_out, lanes, far)
    rows, cols = far.shape
    outs = [like((rows // pieces, cols), BF)] * pieces
    return launch(
        functools.partial(merge_kernel, experts),
        "merge_rows",
        args,
        [scalar_spec()] + [whole(x.shape) for x in args[1:]],
        outs,
        [whole(o.shape) for o in outs],
        math.prod(far.shape),
    )


def shared_kernel(group, weight, *refs):
    blocks, backs = refs[: 2 * group], refs[2 * group : 3 * group]
    back_pre, hidden, rows = refs[3 * group :]
    width, units = weight.shape[0], weight.shape[1] // 2
    fill(rows, blocks, slice(0, width))
    gate_pre = dot(rows[...], weight[:, :units])
    up_pre = dot(rows[...], weight[:, units:])
    sig = jax.nn.sigmoid(gate_pre)
    act = gate_pre * sig
    hidden[...] = (act * up_pre).astype(BF)
    size = backs[0].shape[0]
    for g, back in enumerate(backs):
        span = slice(g * size, (g + 1) * size)
        grad = back[...]
        slope = up_pre[span] * sig[span] * (1.0 + gate_pre[span] * (1.0 - sig[span]))
        back_pre[span, :units] = (grad * slope).astype(BF)
        back_pre[span, units:] = (grad * act[span]).astype(BF)


def shared_chunk(blocks, weight, backs):
    rows = sum(x.shape[0] for x in blocks)
    units = weight.shape[1]
    args = (weight, *blocks, *backs)
    outs = [like((rows, units), BF), like((rows, units // 2), BF)]
    return launch(
        functools.partial(shared_kernel, len(backs)),
        "shared_chunk",
        args,
        [whole(x.shape) for x in args],
        outs,
        [whole(o.shape) for o in outs],
        2 * rows * weight.shape[0] * units,
        scratch=[pltpu.VMEM((rows, weight.shape[0]), BF)],
    )


def combine_kernel(slots, count, group, ids, *refs):
    ranked, parts = refs[: 2 * group], refs[2 * group : 2 * group + count]
    rest = refs[2 * group + count :]
    hidden, weight_out, back_pre, weight_in = rest[:4]
    nears, fars, (rows, ranks) = rest[4 : 4 + group], rest[4 + group : 4 + 2 * group], rest[-2:]
    width = weight_in.shape[0]
    fill(rows, parts, slice(None))
    half = nears[0].shape[0]
    for g in range(group):
        fill(ranks, ranked[2 * g : 2 * g + 2], slice(None))
        choose = choose_slots(ids, slots, ranks[...], g, group)
        mine = slice(2 * g * half, 2 * (g + 1) * half)
        for cols in spans(rows.shape[1], TILE):
            value = dot(choose, rows[:, cols])
            if cols.stop <= width:
                value = value + dot_nt(hidden[mine, :], weight_out[cols, :])
            elif cols.stop <= 2 * width:
                there = slice(cols.start - width, cols.stop - width)
                value = value + dot_nt(back_pre[mine, :], weight_in[there, :])
            nears[g][:, cols] = value[:half]
            fars[g][:, cols] = value[half:].astype(BF)


def combine_rows(ids, slots, ranked, parts, hidden, weight_out, back_pre, weight_in):
    half, width = ranked[0].shape[0], weight_in.shape[0]
    group = len(ranked) // 2
    total = sum(p.shape[0] for p in parts)
    cols = parts[0].shape[1]
    outs = [like((half, cols), F32)] * group + [like((half, cols), BF)] * group
    rest = (hidden, weight_out, back_pre, weight_in)
    result = launch(
        functools.partial(combine_kernel, slots, len(parts), group),
        "combine_rows",
        (ids, *ranked, *parts, *rest),
        [scalar_spec()]
        + [rank_spec(half, width)] * (2 * group)
        + [whole(x.shape) for x in (*parts, *rest)],
        outs,
        [whole(o.shape) for o in outs],
        4 * group * half * (total * cols + (hidden.shape[1] + back_pre.shape[1]) * width),
        scratch=[pltpu.VMEM((total, cols), BF), pltpu.VMEM((2 * half, LANES), BF)],
    )
    return list(zip(result[:group], result[group:]))


def weight_grad_kernel(count, units, pairs, *refs):
    outs = refs[-len(pairs) :]
    for out, (left, right) in zip(outs, pairs):
        total = None
        for k in range(count):
            part = dot_tn(refs[left * count + k][:, :units], refs[right * count + k][...])
            total = part if total is None else total + part
        out[...] = total


def weight_grads(lefts, rights, pairs, units):
    count = len(rights[0])
    rows, width = rights[0][0].shape
    tile = 256
    args = [x for group in (*lefts, *rights) for x in group]
    return launch(
        functools.partial(weight_grad_kernel, count, units, pairs),
        "weight_grads",
        args,
        [whole(x.shape) for group in lefts for x in group]
        + [pl.BlockSpec((rows, tile), lambda i: (0, i))] * (count * len(rights)),
        [like((units, width), F32)] * len(pairs),
        [pl.BlockSpec((units, tile), lambda i: (0, i))] * len(pairs),
        2 * len(pairs) * count * rows * width * units,
        grid=(width // tile,),
    )


def placed(plane, parts):
    n_ctx = len(parts) // 2
    half = parts[0].shape[0]
    for i, part in enumerate(parts):
        block = (i // n_ctx) * n_ctx + (plane[0] ^ (i % n_ctx))
        yield part, pl.ds(pl.multiple_of(block * half, half), half)


def norm_kernel(count, plane, *refs):
    parts, (gain, out) = refs[:count], refs[count:]
    for part, rows in placed(plane, parts):
        out[rows, :] = rmsnorm(part[...].astype(F32), gain[...]).astype(BF)


def norm_rows(plane, parts, gain):
    total = sum(p.shape[0] for p in parts)
    width = parts[0].shape[1]
    gain = gain.reshape(1, width)
    return launch(
        functools.partial(norm_kernel, len(parts)),
        "norm_rows",
        (plane, *parts, gain),
        [scalar_spec()] + [whole(p.shape) for p in parts] + [whole(gain.shape)],
        [like((total, width), BF)],
        [whole((total, width))],
        4 * total * width,
    )[0]


def attended_kernel(count, plane, *refs):
    parts, (weight, attended, back, grad, total) = refs[:count], refs[count:]
    for part, rows in placed(plane, parts):
        total[rows, :] = part[...]
    back[...] = dot_nt(total[...], weight[...]).astype(BF)
    for cols in spans(total.shape[1], TILE):
        grad[:, cols] = dot_tn(attended[...], total[:, cols]).astype(BF)


def attended_back(plane, parts, weight, attended):
    total, cols = attended.shape
    width = weight.shape[1]
    outs = [like((total, cols), BF), like((cols, width), BF)]
    return launch(
        functools.partial(attended_kernel, len(parts)),
        "attended_back",
        (plane, *parts, weight, attended),
        [scalar_spec()]
        + [whole(p.shape) for p in parts]
        + [whole(weight.shape), whole(attended.shape)],
        outs,
        [whole(o.shape) for o in outs],
        4 * total * cols * width,
        scratch=[pltpu.VMEM((total, width), BF)],
    )


def shared_grad_kernel(count, groups, *refs):
    xs, cots = refs[:count], refs[count : 2 * count]
    backs, hiddens = refs[2 * count : 2 * count + groups], refs[2 * count + groups :][:groups]
    out = refs[-1]
    half = xs[0].shape[0]
    each = count // groups
    first = backs[0].shape[1]
    for cols, lefts, rights in (
        (slice(0, first), xs, backs),
        (slice(first, out.shape[1]), cots, hiddens),
    ):
        total = None
        for i, left in enumerate(lefts):
            row = (i % each) * half
            part = dot_tn(left[...], rights[i // each][row : row + half, :])
            total = part if total is None else total + part
        out[:, cols] = total.astype(BF)


def shared_grads(xs, cots, backs, hiddens, width):
    half = xs[0].shape[0]
    tile = 256
    cols = backs[0].shape[1] + hiddens[0].shape[1]
    return launch(
        functools.partial(shared_grad_kernel, len(xs), len(backs)),
        "shared_grads",
        (*xs, *cots, *backs, *hiddens),
        [pl.BlockSpec((half, tile), lambda i: (0, i))] * (len(xs) + len(cots))
        + [whole(b.shape) for b in (*backs, *hiddens)],
        [like((width, cols), BF)],
        [pl.BlockSpec((tile, cols), lambda i: (i, 0))],
        2 * len(xs) * half * width * cols,
        grid=(width // tile,),
    )[0]


def body(
    n_dp,
    n_ctx,
    tokens,
    cotangent,
    lengths,
    deal_order,
    routes,
    attn_gain,
    q_weight,
    kv_down,
    latent_gain,
    kv_up,
    out_weight,
    ffn_gain,
    router,
    shared_gate,
    shared_up,
    shared_down,
    expert_gate,
    expert_up,
    expert_down,
):
    rows, width = tokens.shape
    half = rows // 2
    top = routes.shape[1]
    experts = router.shape[1]
    blocks = n_dp * n_ctx
    band = width // blocks
    slots = 4 * rows * top // (3 * experts) // 2
    z = lax.axis_index("dp")
    c = lax.axis_index("ctx")
    t = lax.axis_index("tp")
    expert_id = z * n_ctx + c
    width_qk = NOPE + ROPE
    width_kv = NOPE + VDIM
    scale_factor = width_qk ** (-0.5)
    heads = q_weight.shape[1] // width_qk // n_ctx
    pack = rows * n_ctx

    def across(x, j):
        return lax.ppermute(x, "ctx", [(i, i ^ j) for i in range(n_ctx)])

    def swap(x):
        return lax.ppermute(x, "tp", [(0, 1), (1, 0)])

    def hop(x):
        return lax.ppermute(x, "dp", [(i, (i + 1) % n_dp) for i in range(n_dp)])

    def own_half(x):
        return lax.dynamic_slice_in_dim(x, t * half, half)

    def both_halves(x):
        other = swap(x)
        first = t == 0
        return jnp.concatenate([jnp.where(first, x, other), jnp.where(first, other, x)], axis=0)

    def gather_parts(x, *marks):
        near = [x] + after([across(x, j) for j in range(1, n_ctx)], *marks)
        return near + [swap(p) for p in near]

    def scatter_pack(near, far):
        near = (near + swap(far).astype(F32)).astype(BF)
        sent = near.reshape(n_ctx, half, near.shape[1])
        return lax.all_to_all(sent, "ctx", split_axis=0, concat_axis=0, tiled=True), sent

    def gathered(parts, *marks):
        return jnp.sum(after(parts, *marks).astype(F32), axis=0)

    def after(values, *marks):
        return lax.optimization_barrier((values, *marks))[0]

    q_cols, out_rows = heads * width_qk, heads * VDIM
    up_cols = heads * width_kv
    up_rows = kv_up.shape[0]
    folds = up_cols // LANES
    lead_cols = q_cols + LANES
    nope_cols = heads * NOPE

    def plane_order(near):
        bit = 1
        while bit < n_ctx:
            shape = near.shape
            pairs = near.reshape((n_ctx // (2 * bit), 2, bit) + shape[1:])
            near = jnp.where((c & bit) > 0, pairs[:, ::-1], pairs).reshape(shape)
            bit *= 2
        return near

    def ring_of(x):
        ring = [x]
        for _ in range(n_dp - 1):
            ring.append(hop(ring[-1]))
        return ring

    def collect(ring, take, block):
        total = None
        for k, x in enumerate(ring):
            part = take(x)
            if total is None:
                total = jnp.zeros((n_dp * block,) + part.shape[1:], part.dtype)
            total = lax.dynamic_update_slice_in_dim(total, part, ((z - k) % n_dp) * block, 0)
        return total

    small = jnp.concatenate([attn_gain, ffn_gain, latent_gain, router.reshape(band * experts)])
    small_rows = -(-small.shape[0] // lead_cols)
    small = jnp.pad(small, (0, small_rows * lead_cols - small.shape[0]))
    small = small.reshape(small_rows, lead_cols)

    def lead_piece(j):
        q = lax.dynamic_slice_in_dim(q_weight, (c ^ j) * q_cols, q_cols, 1)
        q = q.reshape(band, heads, width_qk)
        q = jnp.concatenate(
            [q[..., :NOPE].reshape(band, nope_cols), q[..., NOPE:].reshape(band, -1)], axis=1
        )
        up = lax.dynamic_slice_in_dim(kv_up, (c ^ j) * up_cols, up_cols, 1)
        up = up.reshape(up_rows, folds, LANES).transpose(1, 0, 2).reshape(folds * up_rows, LANES)
        return jnp.concatenate([jnp.concatenate([q, up], axis=1), small], axis=0)

    def out_piece(j):
        return lax.dynamic_slice_in_dim(out_weight, (c ^ j) * out_rows, out_rows, 0)

    lead = [lead_piece(0)] + [across(lead_piece(j), j) for j in range(1, n_ctx)]
    lead = plane_order(jnp.stack(lead))
    own_tokens_low = own_half(tokens)
    token_parts = gather_parts(after(own_tokens_low, lead))
    lead_ring = ring_of(lead)
    q_mine = collect(lead_ring, lambda x: x[:, :band, :q_cols].reshape(-1, q_cols), n_ctx * band)
    up_mine = collect(
        lead_ring,
        lambda x: x[:, :band, q_cols:]
        .reshape(n_ctx, folds, up_rows, LANES)
        .transpose(0, 2, 1, 3)
        .reshape(n_ctx * up_rows, up_cols),
        n_ctx * up_rows,
    )
    small_all = collect(lead_ring, lambda x: x[:, band:], n_ctx).reshape(blocks, -1)
    attn_gain_all = small_all[:, :band].reshape(width).astype(F32)
    ffn_gain_all = small_all[:, band : 2 * band].reshape(width).astype(F32)
    latent_cols = latent_gain.shape[0]
    latent_gain_all = (
        small_all[:, 2 * band : 2 * band + latent_cols].reshape(KV_RANK).astype(F32)
    )
    router_all = small_all[:, 2 * band + latent_cols : 2 * band + latent_cols + band * experts]
    router_all = router_all.reshape(width, experts)

    down_half = lax.dynamic_slice_in_dim(kv_down, t * (band // 2), band // 2)
    down_all = lax.all_gather(down_half, ("dp", "ctx", "tp"), axis=0, tiled=True)

    out_near = plane_order(
        jnp.stack([out_piece(0)] + [across(after(out_piece(j), q_mine), j) for j in range(1, n_ctx)])
    )
    out_mine = (
        lax.all_gather(out_near, "dp", axis=0, tiled=True)
        .transpose(1, 0, 2)
        .reshape(out_rows, width)
    )

    groups = -(-shared_gate.shape[1] // (LANES * n_dp))
    hidden_units = groups * LANES
    all_units = hidden_units * n_dp

    def widen(x, cols):
        return jnp.pad(x, ((0, 0), (0, cols - x.shape[1])))

    def unit_pieces(w):
        return widen(w, all_units).reshape(band, n_dp, hidden_units).transpose(1, 0, 2)

    units = expert_gate.shape[2]
    padded_units = -(-units // 256) * 256
    gate_w, up_w, expert_out = (
        after(jnp.pad(w, ((0, padded_units - units), (0, 0))), lead_ring[1])
        for w in (expert_gate[0].T, expert_up[0].T, expert_down[0])
    )

    plane = c.astype(jnp.int32).reshape(1)
    order_index = jnp.arange(n_ctx)[None, :] * 2 + (t ^ jnp.arange(2))[:, None]
    order_row = deal_order[0].reshape(n_ctx * 2, half)[order_index.reshape(-1)].reshape(pack)
    docs, pos = places(lengths[0], order_row)
    cos_table, sin_table = rope_tables(pos)
    own_cot = own_half(cotangent)
    expert_row = jnp.arange(experts, dtype=jnp.int32)
    hot = jnp.sum((routes[:, :, None] == expert_row[None, None, :]).astype(BF), axis=1)
    row_index = jnp.arange(rows)
    earlier = (row_index[:, None] >= row_index[None, :]).astype(BF)
    rank = dot(earlier, hot) * hot.astype(F32)

    cot_extended = jnp.concatenate(
        [own_cot, own_half(rank).astype(BF), jnp.zeros((half, LANES - experts), BF)], axis=1
    )
    ids = jnp.concatenate(
        [
            (z * n_ctx + jnp.arange(n_ctx, dtype=jnp.int32)).astype(jnp.int32),
            (t * slots + 1).astype(jnp.int32).reshape(1),
        ]
    )

    apart = n_ctx if slots % 16 == 0 else 1
    near_ids = ids
    if apart > 1:
        near_ids = jnp.concatenate(
            [(z * n_ctx + (c ^ jnp.arange(n_ctx, dtype=jnp.int32))).astype(jnp.int32), ids[n_ctx:]]
        )

    def exchange(x):
        total, cols = x.shape
        x = x.reshape(n_ctx, total // n_ctx, cols)
        x = lax.all_to_all(x, "ctx", split_axis=0, concat_axis=0, tiled=True)
        return x.reshape(total, cols)

    def send_slots(parts):
        if apart == 1:
            return [exchange(parts[0])]
        return [parts[0]] + [across(parts[j], j) for j in range(1, n_ctx)]

    def both_cores(parts):
        return parts + [swap(p) for p in parts]

    cot_pairs, cot_parts = [], []

    def cot_step(x):
        pair = (x, swap(x))
        picked = pick_rows(near_ids, slots, pair, pair, width, width, apart)
        cot_pairs.append(pair)
        cot_parts.append(send_slots(picked))

    cot_step(cot_extended)
    normed_low = norm_rows(plane, after(token_parts, cot_parts[0]), attn_gain_all)
    query_pre = dot(normed_low, q_mine)
    query_turned = rotate(
        query_pre[:, nope_cols:].reshape(pack, heads, ROPE),
        cos_table[:, None],
        sin_table[:, None],
    )
    latent_pre = dot(normed_low, down_all)
    latent_low = rmsnorm(latent_pre[:, :KV_RANK], latent_gain_all).astype(BF)
    rope_low = rotate(latent_pre[:, KV_RANK:], cos_table, sin_table).astype(BF)
    if n_dp > 1:
        cot_step(after(hop(after(cot_extended, q_mine)), latent_low))
    expanded = dot(latent_low, up_mine).astype(BF)
    allowed = (docs[:, None] == docs[None, :]) & (pos[None, :] <= pos[:, None])
    queries, keys, values, log_totals, attended = [], [], [], [], []

    def scores_of(h):
        return jnp.where(allowed, dot_nt(queries[h], keys[h]) * scale_factor, NEGATIVE)

    for h in range(heads):
        queries.append(
            jnp.concatenate(
                [query_pre[:, h * NOPE : (h + 1) * NOPE], query_turned[:, h]], axis=1
            ).astype(BF)
        )
        base = h * width_kv
        keys.append(jnp.concatenate([expanded[:, base : base + NOPE], rope_low], axis=1))
        values.append(expanded[:, base + NOPE : base + width_kv])
        scores = scores_of(h)
        highest = jnp.max(scores, axis=-1, keepdims=True)
        exponentials = jnp.exp(scores - highest)
        totals = jnp.sum(exponentials, axis=-1, keepdims=True)
        log_totals.append(highest + jnp.log(totals))
        attended.append(dot((exponentials / totals).astype(BF), values[h]).astype(BF))
    first_attended = attended[0]

    attended = jnp.concatenate(attended, axis=1)
    own_tokens = own_tokens_low.astype(F32)
    middle = pack // 2
    attended = after(attended, cot_parts[-1])
    attended_far = dot(attended[middle:], out_mine).astype(BF)
    attended_parts, attended_sent = scatter_pack(dot(attended[:middle], out_mine), attended_far)

    if n_dp > 2:
        cot_step(after(hop(cot_pairs[1][0]), attended_sent))
    order = list(range(1, n_dp)) + [0]
    groups = [tuple(order[i : i + 2]) for i in range(0, n_dp, 2)]

    def cot_pieces(group):
        if apart > 1:
            return [cot_parts[k][j] for j in range(n_ctx) for k in group]
        near = [cot_parts[k][0].reshape(n_ctx, slots, width) for k in group]
        return [jnp.stack(near, axis=1).reshape(-1, width)]

    hidden_one = own_tokens + gathered(attended_parts, gate_w, up_w)
    for k in range(3, n_dp):
        cot_step(after(hop(cot_pairs[k - 1][0]), attended_sent))

    ffn_normed, ffn_norm_back = jax.vjp(rmsnorm, hidden_one, ffn_gain_all)
    ffn_low = ffn_normed.astype(BF)
    router_probs = jax.nn.softmax(dot(ffn_low, router_all), axis=-1)
    probs_high, probs_low = two_parts(router_probs)
    spare = jnp.zeros((half, LANES - 2 * experts), BF)
    ffn_ring = ring_of(jnp.concatenate([ffn_low, probs_high, probs_low, spare], axis=1))
    shared_send = jnp.concatenate(
        [unit_pieces(w)
            for w in after((shared_gate, shared_up, shared_down.T), ffn_ring[min(2, n_dp - 1)])], axis=2
    )
    shared_part = lax.all_to_all(
        shared_send, "dp", split_axis=0, concat_axis=0, tiled=True
    )
    shared_all = (
        lax.all_gather(shared_part, "ctx", axis=0, tiled=False)
        .transpose(1, 0, 2, 3)
        .reshape(width, 3 * hidden_units)
    )
    shared_in = shared_all[:, : 2 * hidden_units]
    shared_out_t = shared_all[:, 2 * hidden_units :]
    first = jnp.stack([expert_id, c]).astype(jnp.int32)

    mark = [attended_sent]

    def in_turn(run, args, *rest):
        result = run(*after(args, mark[0]), *rest)
        mark[0] = result[0] if isinstance(result, (list, tuple)) else result
        return result

    products = {}
    pairs, x_near, x_in, shared_hidden, back_shared_pre = {}, {}, {}, {}, {}
    nears, fars, returned, combined = {}, {}, {}, {}
    x_rows, back_gates, back_ups, gated = [], [], [], []

    def product_chunk(group):
        products[group] = in_turn(
            lambda *near: cot_product(both_cores(list(near)), expert_out), cot_pieces(group)
        )

    def ranked_of(group):
        return [x for k in group for x in cot_pairs[k]]

    def pick_chunk(group):
        pairs[group] = [x for k in group for x in (ffn_ring[k], swap(ffn_ring[k]))]
        picked = in_turn(
            lambda *blocks: pick_rows(
                near_ids, slots, ranked_of(group), blocks, width, width + LANES, apart
            ),
            pairs[group],
        )
        x_near[group] = send_slots(picked)

    def share_chunk(group):
        back_shared_pre[group], shared_hidden[group] = in_turn(
            lambda *blocks: shared_chunk(blocks, shared_in, [back_shared[k] for k in group]),
            pairs[group],
        )

    def run_expert(group):
        x, back_gate, back_up, gated_hidden, *near, far = in_turn(
            lambda *parts: expert_chunk(
                list(parts), experts, first, products[group][0], gate_w, up_w, expert_out
            ),
            x_in[group],
        )
        x_rows.append(x)
        back_gates.append(back_gate)
        back_ups.append(back_up)
        gated.append(gated_hidden)
        nears[group] = near
        fars[group] = swap(far)

    def merge_chunk(group):
        merged = in_turn(
            lambda *parts: merge_rows(experts, apart, first, *parts),
            (*nears[group], fars[group]),
        )
        returned[group] = send_slots(merged)

    def combine_chunk(group):
        sums = in_turn(
            lambda *parts: combine_rows(
                near_ids,
                slots,
                ranked_of(group),
                parts,
                shared_hidden[group],
                shared_out_t,
                back_shared_pre[group],
                shared_in,
            ),
            returned[group],
        )
        combined.update(zip(group, sums))

    product_chunk(groups[0])
    pick_chunk(groups[0])
    for p, group in enumerate(groups):
        x_in[group] = both_cores(after(x_near[group], mark[0]))
        if p + 1 < len(groups):
            pick_chunk(groups[p + 1])
        run_expert(group)
        if p == 0:
            back_shared = in_turn(
                lambda *flat: cot_shared(
                    [flat[2 * i : 2 * i + 2] for i in range(n_dp)], shared_out_t
                ),
                [x for pair in cot_pairs for x in pair],
            )
            share_chunk(group)
        else:
            combine_chunk(groups[p - 1])
        merge_chunk(group)
        if p + 1 < len(groups):
            product_chunk(groups[p + 1])
            share_chunk(groups[p + 1])
    cot_rows = [products[group][1] for group in groups]
    shared_backs = [back_shared_pre[group] for group in groups]
    shared_hiddens = [shared_hidden[group] for group in groups]
    grad_egate, grad_eup = in_turn(
        lambda *gates: weight_grads([gates, back_ups], [x_rows], ((0, 2), (1, 2)), units),
        back_gates,
    )
    x_pairs = [x for group in groups for x in pairs[group]]
    cot_flat = [x for group in groups for x in ranked_of(group)]
    totals = []

    def add_chunk(k):
        near, far = combined[k]
        near = near + swap(far).astype(F32)
        if totals:
            moved = hop(totals[-1].astype(BF))
            near = near + (after(moved, grad_egate) if k in order[:-2] else moved).astype(F32)
        totals.append(near)

    for k in order[:-2]:
        add_chunk(k)
    if totals:
        mark[0] = (mark[0], totals[-1])
    grad_shared = in_turn(
        lambda *xs: shared_grads(xs, cot_flat, shared_backs, shared_hiddens, width), x_pairs
    )
    grad_shared = grad_shared.reshape(n_dp, n_ctx, band, 3 * hidden_units)
    grad_shared = grad_shared.transpose(1, 0, 2, 3).reshape(width, 3 * hidden_units)
    mark[0] = grad_shared
    combine_chunk(groups[-1])
    for k in order[-2:]:
        add_chunk(k)
    total = totals[-1]
    output_sum, back_ffn = total[:, :width], total[:, width:]
    back_probs = (
        back_ffn[:, width : width + experts] + back_ffn[:, width + experts : width + 2 * experts]
    )
    back_logits = router_probs * (
        back_probs - jnp.sum(router_probs * back_probs, axis=-1, keepdims=True)
    )
    back_ffn_normed = back_ffn[:, :width] + jnp.dot(
        back_logits, router_all.astype(F32).T, precision=PRECISE
    )
    grad_router = jnp.dot(back_logits.T, ffn_low.astype(F32), precision=PRECISE)
    back_hidden_one, grad_ffn_gain = ffn_norm_back(back_ffn_normed)
    back_hidden_one = back_hidden_one + own_cot.astype(F32)

    mark[0] = back_hidden_one
    (grad_edown,) = in_turn(
        lambda *gates: weight_grads([gates], [cot_rows], ((0, 1),), units), gated
    )
    back_parts = gather_parts(back_hidden_one.astype(BF), grad_edown)
    output = both_halves((hidden_one + output_sum).astype(BF))

    back_attended, grad_out_t = attended_back(plane, back_parts, out_mine, attended)
    grad_shared = lax.psum_scatter(
        after(grad_shared, back_parts), "ctx", scatter_dimension=0, tiled=True
    )
    grad_out_t = lax.psum_scatter(grad_out_t, "dp", scatter_dimension=1, tiled=True)
    back_nope, back_turned, back_expanded, back_rope = [], [], [], None
    for h in range(heads):
        back_head = back_attended[:, h * VDIM : (h + 1) * VDIM]
        probabilities = jnp.exp(scores_of(h) - log_totals[h])
        back_prob = dot_nt(back_head, values[h])
        inner_sum = jnp.sum(probabilities * back_prob, axis=-1, keepdims=True)
        back_raw = (probabilities * (back_prob - inner_sum) * scale_factor).astype(BF)
        back_query = dot(back_raw, keys[h])
        back_key = dot_tn(back_raw, queries[h])
        back_nope.append(back_query[:, :NOPE].astype(BF))
        back_turned.append(unrotate(back_query[:, NOPE:], cos_table, sin_table).astype(BF))
        back_expanded.append(back_key[:, :NOPE].astype(BF))
        back_expanded.append(dot_tn(probabilities.astype(BF), back_head).astype(BF))
        turned = back_key[:, NOPE:]
        back_rope = turned if back_rope is None else back_rope + turned
    grad_shared_sum = grad_shared
    grad_shared = grad_shared.reshape(n_dp, band, 3 * hidden_units)
    shared_near = [lax.dynamic_index_in_dim(grad_shared, z, 0, keepdims=False)]
    for i in range(1, n_dp):
        sent = lax.dynamic_index_in_dim(grad_shared, (z + i) % n_dp, 0, keepdims=False)
        shared_near.append(
            lax.ppermute(sent, "dp", [(a, (a + i) % n_dp) for a in range(n_dp)])
        )
    grad_shared = shared_near
    back_nope = after(back_nope, grad_shared_sum)
    back_query_pre = jnp.concatenate(back_nope + back_turned, axis=1)
    back_expanded = jnp.concatenate(back_expanded, axis=1)
    back_latent = jnp.concatenate(
        [dot_nt(back_expanded, up_mine), back_rope, jnp.zeros((pack, ROPE), F32)], axis=1
    )
    latent_near = back_latent[:middle] + swap(back_latent[middle:].astype(BF)).astype(F32)
    latent_near = latent_near.astype(BF).reshape(n_ctx, half, -1)
    latent_parts = jnp.stack(
        [lax.dynamic_index_in_dim(latent_near, c, 0, keepdims=False)]
        + [
            across(lax.dynamic_index_in_dim(latent_near, c ^ j, 0, keepdims=False), j)
            for j in range(1, n_ctx)
        ]
    )
    grad_heads = jnp.concatenate(
        [
            dot_tn(normed_low, back_query_pre),
            dot_tn(latent_low, back_expanded)
            .reshape(blocks, up_rows, folds, LANES)
            .transpose(0, 2, 1, 3)
            .reshape(width, LANES),
        ],
        axis=1,
    ).astype(BF)
    back_query_pre = after(back_query_pre, grad_heads)
    back_far = dot_nt(back_query_pre[middle:], q_mine).astype(BF)
    back_near = dot_nt(back_query_pre[:middle], q_mine) + swap(back_far).astype(F32)
    back_near = back_near.astype(BF).reshape(n_ctx, half, width)
    back_sent = [
        lax.dynamic_index_in_dim(back_near, c ^ j, 0, keepdims=False) for j in range(n_ctx)
    ]
    back_sum_parts = [back_sent[0]] + [across(back_sent[j], j) for j in range(1, n_ctx)]
    back_latent = gathered(latent_parts, back_sent)
    own_rows = functools.partial(lax.dynamic_slice_in_dim, start_index=c * half, slice_size=half)
    own_latent = own_rows(latent_pre)[:, :KV_RANK]
    back_latent_pre, grad_latent_gain = jax.vjp(rmsnorm, own_latent, latent_gain_all)[1](
        back_latent[:, :KV_RANK]
    )
    back_down = jnp.concatenate(
        [
            back_latent_pre,
            unrotate(
                back_latent[:, KV_RANK : KV_RANK + ROPE], own_rows(cos_table), own_rows(sin_table)
            ),
        ],
        axis=1,
    ).astype(BF)
    back_near = plane_order(
        jnp.stack([back_down] + [across(back_down, j) for j in range(1, n_ctx)])
    )
    back_near = back_near.reshape(middle, back_down.shape[1])
    back_down_parts = [back_near, swap(back_near)]
    back_sum = sum(x.astype(F32) for x in back_sum_parts)
    back_normed = back_sum + dot_nt(back_down, down_all)
    back_inputs, grad_attn_gain = jax.vjp(rmsnorm, own_tokens, attn_gain_all)[1](back_normed)
    input_grad = both_halves(back_hidden_one + back_inputs)

    placed_shared = jnp.zeros((n_dp, band, 3 * hidden_units), F32)
    for i, part in enumerate(after(grad_shared, back_sent)):
        placed_shared = lax.dynamic_update_index_in_dim(
            placed_shared, part.astype(F32), (z - i) % n_dp, 0
        )
    grad_sgate, grad_sup, grad_sdown = (
        placed_shared[:, :, i * hidden_units : (i + 1) * hidden_units]
        .transpose(1, 0, 2)
        .reshape(band, all_units)[:, : shared_gate.shape[1]]
        for i in range(3)
    )

    grad_heads = lax.psum_scatter(grad_heads, "dp", scatter_dimension=0, tiled=True)
    grad_heads = lax.all_to_all(
        after(grad_heads, back_sum_parts).reshape(n_ctx, band, -1), "ctx", split_axis=0, concat_axis=0, tiled=True
    ).astype(F32)
    grad_q = jnp.concatenate(
        [
            grad_heads[:, :, :nope_cols].reshape(n_ctx, band, heads, NOPE),
            grad_heads[:, :, nope_cols:q_cols].reshape(n_ctx, band, heads, ROPE),
        ],
        axis=3,
    )
    grad_q = grad_q.transpose(1, 0, 2, 3).reshape(band, n_ctx * q_cols)
    grad_out = lax.all_to_all(
        after(grad_out_t, back_sum).reshape(out_rows, n_ctx, band).transpose(1, 0, 2),
        "ctx",
        split_axis=0,
        concat_axis=0,
        tiled=True,
    )
    grad_out = grad_out.astype(F32).reshape(n_ctx * out_rows, band)
    grad_up = (
        grad_heads[:, :, q_cols:]
        .reshape(n_ctx, folds, up_rows, LANES)
        .transpose(2, 0, 1, 3)
        .reshape(up_rows, n_ctx * up_cols)
    )
    back_down_pack = jnp.concatenate(back_down_parts, axis=0)
    normed_band = jnp.concatenate(
        [
            lax.dynamic_slice_in_dim(normed_low, (i * n_ctx + c) * band, band, axis=1)
            for i in range(n_dp)
        ],
        axis=1,
    )
    down_sums = dot_tn(normed_band, back_down_pack).reshape(n_dp, band, -1)
    grad_down = lax.dynamic_index_in_dim(down_sums, z, 0, keepdims=False)
    for i in range(1, n_dp):
        sent = lax.dynamic_index_in_dim(down_sums, (z + i) % n_dp, 0, keepdims=False)
        sent = lax.ppermute(sent.astype(BF), "dp", [(a, (a + i) % n_dp) for a in range(n_dp)])
        grad_down = grad_down + sent.astype(F32)
    late = jnp.concatenate(
        [
            grad_router.reshape(experts, blocks, band).transpose(1, 0, 2),
            grad_ffn_gain.reshape(blocks, 1, band),
            grad_attn_gain.reshape(blocks, 1, band),
            widen(grad_latent_gain.reshape(blocks, latent_cols), band)[:, None],
        ],
        axis=1,
    )
    late = jnp.sum(
        lax.all_to_all(late + swap(late), GRID, split_axis=0, concat_axis=0, tiled=True), axis=0
    )
    return (
        output,
        input_grad,
        late[experts + 1],
        grad_q,
        grad_down,
        late[experts + 2, :latent_cols],
        grad_up,
        grad_out,
        late[experts],
        late[:experts].T,
        grad_sgate,
        grad_sup,
        grad_sdown.T,
        grad_egate.T[None],
        grad_eup.T[None],
        grad_edown[None],
    )


def solution(mesh):
    n_dp, n_ctx = mesh.shape["dp"], mesh.shape["ctx"]
    ins = (
        P(GRID, None),
        P(GRID, None),
        P("dp", None),
        P("dp", None),
        P(GRID, None),
        P(GRID),
        P(GRID, "tp"),
        P(GRID, None),
        P(GRID),
        P(GRID, "tp"),
        P("tp", GRID),
        P(GRID),
        P(GRID, None),
        P(GRID, "tp"),
        P(GRID, "tp"),
        P("tp", GRID),
        P(GRID, None, "tp"),
        P(GRID, None, "tp"),
        P(GRID, "tp", None),
    )
    outs = (
        P(GRID, None),
        P(GRID, None),
        P(GRID),
        P(GRID, "tp"),
        P(GRID, None),
        P(GRID),
        P(GRID, "tp"),
        P("tp", GRID),
        P(GRID),
        P(GRID, None),
        P(GRID, "tp"),
        P(GRID, "tp"),
        P("tp", GRID),
        P(GRID, None, "tp"),
        P(GRID, None, "tp"),
        P(GRID, "tp", None),
    )
    return jax.shard_map(
        functools.partial(body, n_dp, n_ctx),
        mesh=mesh,
        in_specs=ins,
        out_specs=outs,
        check_vma=False,
    )
```

```python
import functools
import math

import jax
import jax.numpy as jnp
from jax import lax
from jax.experimental import pallas as pl
from jax.experimental.pallas import tpu as pltpu
from jax.sharding import PartitionSpec as P

NOPE = 128
ROPE = 64
VDIM = 128
KV_RANK = 512
LANES = 128

EPSILON = 1e-06
NEGATIVE = -1e30
PRECISE = lax.Precision.HIGHEST
BF = jnp.bfloat16
F32 = jnp.float32
GRID = ("dp", "ctx")


def rmsnorm(values, gain_vec):
    return (
        values * lax.rsqrt(jnp.mean(values * values, axis=-1, keepdims=True) + EPSILON) * gain_vec
    )


def rope_tables(position):
    frequency = jnp.exp(
        jnp.arange(ROPE // 2, dtype=F32) * (-2.0 * math.log(10000.0) / ROPE)
    )
    angle_table = position.astype(F32)[:, None] * frequency[None, :]
    return (jnp.cos(angle_table), jnp.sin(angle_table))


def rotate(values, cos_table, sin_table):
    half_size = values.shape[-1] // 2
    first_half = values[..., :half_size]
    second_half = values[..., half_size:]
    return jnp.concatenate(
        [
            first_half * cos_table - second_half * sin_table,
            first_half * sin_table + second_half * cos_table,
        ],
        axis=-1,
    )


def unrotate(values, cos_table, sin_table):
    return rotate(values, cos_table, -sin_table)


def places(lengths_row, order_row):
    doc_ends = jnp.cumsum(lengths_row)
    starts = doc_ends - lengths_row
    doc_ids = jnp.sum((order_row[:, None] >= doc_ends[None, :]).astype(jnp.int32), axis=1)
    matched = doc_ids[:, None] == jnp.arange(lengths_row.shape[0], dtype=jnp.int32)[None, :]
    doc_start = jnp.sum(jnp.where(matched, starts[None, :], 0), axis=1)
    return (doc_ids, order_row - doc_start)


def dot(left, right):
    return jnp.dot(left, right, preferred_element_type=F32)


def dot_nt(left, right):
    return lax.dot_general(left, right, (((1,), (1,)), ((), ())), preferred_element_type=F32)


def dot_tn(left, right):
    return lax.dot_general(left, right, (((0,), (0,)), ((), ())), preferred_element_type=F32)


def two_parts(values):
    high = lax.reduce_precision(values, 8, 7)
    return high.astype(BF), (values - high).astype(BF)


TILE = 512
EAGER = 16


def whole(shape):
    return pl.BlockSpec(shape, lambda *_: (0,) * len(shape))


def scalar_spec():
    return pl.BlockSpec(memory_space=pltpu.SMEM)


def like(shape, dtype):
    return jax.ShapeDtypeStruct(shape, dtype)


def launch(kernel, name, args, in_specs, outs, out_specs, flops, grid=(1,), scratch=()):
    moved = sum(math.prod(a.shape) * a.dtype.itemsize for a in (*args, *outs))
    return pl.pallas_call(
        kernel,
        grid=grid,
        in_specs=in_specs,
        out_specs=out_specs,
        out_shape=outs,
        scratch_shapes=scratch,
        name=name,
        cost_estimate=pl.CostEstimate(
            flops=flops // EAGER, bytes_accessed=moved // EAGER, transcendentals=0
        ),
    )(*args)


def spans(total, step):
    return [slice(lo, min(lo + step, total)) for lo in range(0, total, step)]


def fill(ref, parts, cols):
    row = 0
    for part in parts:
        size = part.shape[-2]
        value = part[..., cols]
        ref[row : row + size, :] = value.reshape(size, value.shape[-1])
        row += size


def drain(outs, value, cols):
    row = 0
    for out in outs:
        size = out.shape[0]
        out[:, cols] = value[row : row + size]
        row += size


def slot_places(ids, slots, ranks):
    plane = ids.shape[0] - 1
    lane = lax.broadcasted_iota(jnp.int32, (8, LANES), 1)
    sub = lax.broadcasted_iota(jnp.int32, (8, LANES), 0)
    found = jnp.zeros((8, LANES), F32)
    for j in range(plane):
        found = jnp.where((sub == j) & (lane == ids[j]), 1.0, found)
    return found.astype(BF), ids[plane].astype(F32), plane


def within(number, first, slots, base):
    place = number - first
    return jnp.where((place >= 0) & (place < slots), place + base, -1.0)


def choose_rows(ids, slots, ranks, g, group):
    found, first, plane = slot_places(ids, slots, ranks)
    numbers = dot_nt(found, ranks)
    total, rows = plane * group * slots, ranks.shape[0]
    place = lax.broadcasted_iota(jnp.int32, (total, rows), 0).astype(F32)
    chosen = jnp.zeros((total, rows), F32)
    for j in range(plane):
        there = within(numbers[j : j + 1, :], first, slots, (j * group + g) * slots)
        chosen = jnp.where(place == there, 1.0, chosen)
    return chosen.astype(BF)


def choose_slots(ids, slots, ranks, g, group):
    found, first, plane = slot_places(ids, slots, ranks)
    numbers = dot_nt(ranks, found)
    total, rows = plane * group * slots, ranks.shape[0]
    place = lax.broadcasted_iota(jnp.int32, (rows, total), 1).astype(F32)
    chosen = jnp.zeros((rows, total), F32)
    for j in range(plane):
        there = within(numbers[:, j : j + 1], first, slots, (j * group + g) * slots)
        chosen = jnp.where(place == there, 1.0, chosen)
    return chosen.astype(BF)


def pick_kernel(slots, group, ids, *refs):
    ranked, pairs = refs[: 2 * group], refs[2 * group : 4 * group]
    outs, (ranks, rows) = refs[4 * group : -2], refs[-2:]
    cols = rows.shape[1]
    half = ranked[0].shape[0]
    chosen = []
    for g in range(group):
        fill(ranks, ranked[2 * g : 2 * g + 2], slice(None))
        chosen.append(choose_rows(ids, slots, ranks[...], g, group))
        for side in range(2):
            row = (2 * g + side) * half
            rows[row : row + half, :] = pairs[2 * g + side][:, :cols]
    for span in spans(cols, TILE):
        value = None
        for g in range(group):
            part = dot(chosen[g], rows[2 * g * half : 2 * (g + 1) * half, span])
            value = part if value is None else value + part
        drain(outs, value.astype(BF), span)


def rank_spec(half, width):
    return pl.BlockSpec((half, LANES), lambda *_: (0, width // LANES))


def pick_rows(ids, slots, ranked, blocks, width, cols, parts):
    half = blocks[0].shape[0]
    group = len(blocks) // 2
    total = (ids.shape[0] - 1) * slots * group
    outs = [like((total // parts, cols), BF)] * parts
    return launch(
        functools.partial(pick_kernel, slots, group),
        "pick_rows",
        (ids, *ranked, *blocks),
        [scalar_spec()]
        + [rank_spec(half, width)] * (2 * group)
        + [whole((half, cols))] * (2 * group),
        outs,
        [whole(o.shape) for o in outs],
        4 * group * total * half * cols,
        scratch=[
            pltpu.VMEM((2 * half, LANES), BF),
            pltpu.VMEM((2 * group * half, cols), BF),
        ],
    )


def cot_kernel(count, *refs):
    parts, (weight, back, rows) = refs[:count], refs[count:]
    fill(rows, parts, slice(None))
    for cols in spans(weight.shape[0], 256):
        back[:, cols] = dot_nt(rows[...], weight[cols, :])


def cot_product(parts, weight):
    total = sum(p.shape[0] for p in parts)
    units, width = weight.shape
    outs = [like((total, units), F32), like((total, width), BF)]
    return launch(
        functools.partial(cot_kernel, len(parts)),
        "cot_product",
        (*parts, weight),
        [whole(p.shape) for p in parts] + [whole(weight.shape)],
        outs,
        [whole(o.shape) for o in outs],
        2 * total * units * width,
    )


def cot_shared_kernel(count, *refs):
    parts, weight, outs = refs[:count], refs[count], refs[count + 1 :]
    half = parts[0].shape[0]
    for k, part in enumerate(parts):
        row = (k % 2) * half
        outs[k // 2][row : row + half, :] = dot(part[...], weight[...])


def cot_shared(pairs, weight):
    parts = [x for pair in pairs for x in pair]
    half = parts[0].shape[0]
    width, units = weight.shape
    outs = [like((2 * half, units), F32)] * len(pairs)
    return launch(
        functools.partial(cot_shared_kernel, len(parts)),
        "cot_shared",
        (*parts, weight),
        [whole((half, width))] * len(parts) + [whole(weight.shape)],
        outs,
        [whole(o.shape) for o in outs],
        2 * len(parts) * half * units * width,
    )


def lane_masks(first, experts):
    lane = lax.broadcasted_iota(jnp.int32, (1, LANES), 1)
    return lane == first, lane == first + experts


def split_lanes(masks, value):
    high = value.astype(BF).astype(F32)
    return jnp.where(masks[0], high, jnp.where(masks[1], value - high, 0.0))


def expert_kernel(count, experts, tiles, first, *refs):
    parts = refs[:count]
    back, gate_w, up_w, gate_c, up_c, down_c, x, back_gate, back_up, gated = refs[
        count : count + 10
    ]
    near, near_out, lanes_out, far, gate_s, sum_s = refs[count + 10 :]
    step = pl.program_id(0)
    width = gate_w.shape[1]
    middle = near.shape[0]
    tile = gate_w.shape[0]
    masks = lane_masks(first[0], experts)

    @pl.when(step == 0)
    def _():
        fill(x, parts, slice(0, width))
        row = 0
        for part in parts:
            size = part.shape[0]
            lanes = part[:, width:].astype(F32)
            gate = jnp.sum(jnp.where(masks[0] | masks[1], lanes, 0.0), axis=1, keepdims=True)
            gate_s[row : row + size, :] = jnp.broadcast_to(gate, (size, LANES))
            row += size
        sum_s[...] = jnp.zeros_like(sum_s)

    @pl.when(step < tiles)
    def _():
        there = pl.ds(pl.multiple_of(step * tile, tile), tile)
        for rows in spans(x.shape[0], 2 * TILE):
            gate_pre = dot_nt(x[rows, :], gate_w[...])
            up_pre = dot_nt(x[rows, :], up_w[...])
            gate = gate_s[rows, :1]
            back_hidden = back[rows, :]
            sig = jax.nn.sigmoid(gate_pre)
            act = gate_pre * sig
            hidden = act * up_pre
            gated[rows, there] = (gate * hidden).astype(BF)
            total = jnp.sum(hidden * back_hidden, axis=1, keepdims=True)
            sum_s[rows, :] += jnp.broadcast_to(total, (total.shape[0], LANES))
            scaled = gate * back_hidden
            back_up[rows, there] = (scaled * act).astype(BF)
            back_gate[rows, there] = (
                scaled * up_pre * sig * (1.0 + gate_pre * (1.0 - sig))
            ).astype(BF)

    @pl.when(step >= tiles)
    def _():
        cols = gate_c.shape[1]
        start = pl.multiple_of((step - tiles) * cols, cols)
        value = dot(back_gate[...], gate_c[...]) + dot(back_up[...], up_c[...])
        near[...] = value[:middle]
        far[:, pl.ds(width + start, cols)] = value[middle:].astype(BF)
        value = dot(gated[...], down_c[...])
        near_out[...] = value[:middle].astype(BF)
        far[:, pl.ds(start, cols)] = value[middle:].astype(BF)

    @pl.when(step == tiles)
    def _():
        lanes_out[...] = jnp.where(masks[0], sum_s[:middle, :], 0.0)
        far[:, 2 * width :] = split_lanes(masks, sum_s[middle:, :]).astype(BF)


def expert_chunk(parts, experts, first, back, gate_w, up_w, down_w):
    total = sum(p.shape[0] for p in parts)
    units, width = gate_w.shape
    tile, cols = 256, 256
    tiles, steps = units // tile, width // cols
    middle = total // 2
    outs = [
        like((total, width), BF),
        like((total, units), BF),
        like((total, units), BF),
        like((total, units), BF),
        like((middle, width), F32),
        like((middle, width), BF),
        like((middle, LANES), F32),
        like((middle, 2 * width + LANES), BF),
    ]

    def one(i):
        return jnp.minimum(i, tiles - 1)

    def two(i):
        return jnp.maximum(i - tiles, 0)

    return launch(
        functools.partial(expert_kernel, len(parts), experts, tiles),
        "expert_chunk",
        (first, *parts, back, gate_w, up_w, gate_w, up_w, down_w),
        [scalar_spec()]
        + [whole(p.shape) for p in parts]
        + [pl.BlockSpec((total, tile), lambda i: (0, one(i)))]
        + [pl.BlockSpec((tile, width), lambda i: (one(i), 0))] * 2
        + [pl.BlockSpec((units, cols), lambda i: (0, two(i)))] * 3,
        outs,
        [whole(o.shape) for o in outs[:4]]
        + [pl.BlockSpec((middle, cols), lambda i: (0, two(i)))] * 2
        + [whole(o.shape) for o in outs[6:]],
        10 * total * width * units,
        grid=(tiles + steps,),
        scratch=[pltpu.VMEM((total, LANES), F32), pltpu.VMEM((total, LANES), F32)],
    )


def merge_kernel(experts, first, near, near_out, lanes, far, *outs):
    width = near_out.shape[1]
    for cols in spans(width, TILE):
        drain(outs, (near_out[:, cols].astype(F32) + far[:, cols].astype(F32)).astype(BF), cols)
        there = slice(width + cols.start, width + cols.stop)
        drain(outs, (near[:, cols] + far[:, there].astype(F32)).astype(BF), there)
    total = jnp.sum(lanes[...] + far[:, 2 * width :].astype(F32), axis=1, keepdims=True)
    value = split_lanes(lane_masks(first[0], experts), jnp.broadcast_to(total, lanes.shape))
    drain(outs, value.astype(BF), slice(2 * width, 2 * width + LANES))


def merge_rows(experts, pieces, first, near, near_out, lanes, far):
    args = (first, near, near_out, lanes, far)
    rows, cols = far.shape
    outs = [like((rows // pieces, cols), BF)] * pieces
    return launch(
        functools.partial(merge_kernel, experts),
        "merge_rows",
        args,
        [scalar_spec()] + [whole(x.shape) for x in args[1:]],
        outs,
        [whole(o.shape) for o in outs],
        math.prod(far.shape),
    )


def shared_kernel(group, weight, *refs):
    blocks, backs = refs[: 2 * group], refs[2 * group : 3 * group]
    back_pre, hidden, rows = refs[3 * group :]
    width, units = weight.shape[0], weight.shape[1] // 2
    fill(rows, blocks, slice(0, width))
    gate_pre = dot(rows[...], weight[:, :units])
    up_pre = dot(rows[...], weight[:, units:])
    sig = jax.nn.sigmoid(gate_pre)
    act = gate_pre * sig
    hidden[...] = (act * up_pre).astype(BF)
    size = backs[0].shape[0]
    for g, back in enumerate(backs):
        span = slice(g * size, (g + 1) * size)
        grad = back[...]
        slope = up_pre[span] * sig[span] * (1.0 + gate_pre[span] * (1.0 - sig[span]))
        back_pre[span, :units] = (grad * slope).astype(BF)
        back_pre[span, units:] = (grad * act[span]).astype(BF)


def shared_chunk(blocks, weight, backs):
    rows = sum(x.shape[0] for x in blocks)
    units = weight.shape[1]
    args = (weight, *blocks, *backs)
    outs = [like((rows, units), BF), like((rows, units // 2), BF)]
    return launch(
        functools.partial(shared_kernel, len(backs)),
        "shared_chunk",
        args,
        [whole(x.shape) for x in args],
        outs,
        [whole(o.shape) for o in outs],
        2 * rows * weight.shape[0] * units,
        scratch=[pltpu.VMEM((rows, weight.shape[0]), BF)],
    )


def combine_kernel(slots, count, group, ids, *refs):
    ranked, parts = refs[: 2 * group], refs[2 * group : 2 * group + count]
    rest = refs[2 * group + count :]
    hidden, weight_out, back_pre, weight_in = rest[:4]
    nears, fars, (rows, ranks) = rest[4 : 4 + group], rest[4 + group : 4 + 2 * group], rest[-2:]
    width = weight_in.shape[0]
    fill(rows, parts, slice(None))
    half = nears[0].shape[0]
    for g in range(group):
        fill(ranks, ranked[2 * g : 2 * g + 2], slice(None))
        choose = choose_slots(ids, slots, ranks[...], g, group)
        mine = slice(2 * g * half, 2 * (g + 1) * half)
        for cols in spans(rows.shape[1], TILE):
            value = dot(choose, rows[:, cols])
            if cols.stop <= width:
                value = value + dot_nt(hidden[mine, :], weight_out[cols, :])
            elif cols.stop <= 2 * width:
                there = slice(cols.start - width, cols.stop - width)
                value = value + dot_nt(back_pre[mine, :], weight_in[there, :])
            nears[g][:, cols] = value[:half]
            fars[g][:, cols] = value[half:].astype(BF)


def combine_rows(ids, slots, ranked, parts, hidden, weight_out, back_pre, weight_in):
    half, width = ranked[0].shape[0], weight_in.shape[0]
    group = len(ranked) // 2
    total = sum(p.shape[0] for p in parts)
    cols = parts[0].shape[1]
    outs = [like((half, cols), F32)] * group + [like((half, cols), BF)] * group
    rest = (hidden, weight_out, back_pre, weight_in)
    result = launch(
        functools.partial(combine_kernel, slots, len(parts), group),
        "combine_rows",
        (ids, *ranked, *parts, *rest),
        [scalar_spec()]
        + [rank_spec(half, width)] * (2 * group)
        + [whole(x.shape) for x in (*parts, *rest)],
        outs,
        [whole(o.shape) for o in outs],
        4 * group * half * (total * cols + (hidden.shape[1] + back_pre.shape[1]) * width),
        scratch=[pltpu.VMEM((total, cols), BF), pltpu.VMEM((2 * half, LANES), BF)],
    )
    return list(zip(result[:group], result[group:]))


def weight_grad_kernel(count, units, pairs, *refs):
    outs = refs[-len(pairs) :]
    for out, (left, right) in zip(outs, pairs):
        total = None
        for k in range(count):
            part = dot_tn(refs[left * count + k][:, :units], refs[right * count + k][...])
            total = part if total is None else total + part
        out[...] = total


def weight_grads(lefts, rights, pairs, units):
    count = len(rights[0])
    rows, width = rights[0][0].shape
    tile = 256
    args = [x for group in (*lefts, *rights) for x in group]
    return launch(
        functools.partial(weight_grad_kernel, count, units, pairs),
        "weight_grads",
        args,
        [whole(x.shape) for group in lefts for x in group]
        + [pl.BlockSpec((rows, tile), lambda i: (0, i))] * (count * len(rights)),
        [like((units, width), F32)] * len(pairs),
        [pl.BlockSpec((units, tile), lambda i: (0, i))] * len(pairs),
        2 * len(pairs) * count * rows * width * units,
        grid=(width // tile,),
    )


def placed(plane, parts):
    n_ctx = len(parts) // 2
    half = parts[0].shape[0]
    for i, part in enumerate(parts):
        block = (i // n_ctx) * n_ctx + (plane[0] ^ (i % n_ctx))
        yield part, pl.ds(pl.multiple_of(block * half, half), half)


def norm_kernel(count, plane, *refs):
    parts, (gain, out) = refs[:count], refs[count:]
    for part, rows in placed(plane, parts):
        out[rows, :] = rmsnorm(part[...].astype(F32), gain[...]).astype(BF)


def norm_rows(plane, parts, gain):
    total = sum(p.shape[0] for p in parts)
    width = parts[0].shape[1]
    gain = gain.reshape(1, width)
    return launch(
        functools.partial(norm_kernel, len(parts)),
        "norm_rows",
        (plane, *parts, gain),
        [scalar_spec()] + [whole(p.shape) for p in parts] + [whole(gain.shape)],
        [like((total, width), BF)],
        [whole((total, width))],
        4 * total * width,
    )[0]


def attended_kernel(count, plane, *refs):
    parts, (weight, attended, back, grad, total) = refs[:count], refs[count:]
    for part, rows in placed(plane, parts):
        total[rows, :] = part[...]
    back[...] = dot_nt(total[...], weight[...]).astype(BF)
    for cols in spans(total.shape[1], TILE):
        grad[:, cols] = dot_tn(attended[...], total[:, cols]).astype(BF)


def attended_back(plane, parts, weight, attended):
    total, cols = attended.shape
    width = weight.shape[1]
    outs = [like((total, cols), BF), like((cols, width), BF)]
    return launch(
        functools.partial(attended_kernel, len(parts)),
        "attended_back",
        (plane, *parts, weight, attended),
        [scalar_spec()]
        + [whole(p.shape) for p in parts]
        + [whole(weight.shape), whole(attended.shape)],
        outs,
        [whole(o.shape) for o in outs],
        4 * total * cols * width,
        scratch=[pltpu.VMEM((total, width), BF)],
    )


def shared_grad_kernel(count, groups, *refs):
    xs, cots = refs[:count], refs[count : 2 * count]
    backs, hiddens = refs[2 * count : 2 * count + groups], refs[2 * count + groups :][:groups]
    out = refs[-1]
    half = xs[0].shape[0]
    each = count // groups
    first = backs[0].shape[1]
    for cols, lefts, rights in (
        (slice(0, first), xs, backs),
        (slice(first, out.shape[1]), cots, hiddens),
    ):
        total = None
        for i, left in enumerate(lefts):
            row = (i % each) * half
            part = dot_tn(left[...], rights[i // each][row : row + half, :])
            total = part if total is None else total + part
        out[:, cols] = total.astype(BF)


def shared_grads(xs, cots, backs, hiddens, width):
    half = xs[0].shape[0]
    tile = 256
    cols = backs[0].shape[1] + hiddens[0].shape[1]
    return launch(
        functools.partial(shared_grad_kernel, len(xs), len(backs)),
        "shared_grads",
        (*xs, *cots, *backs, *hiddens),
        [pl.BlockSpec((half, tile), lambda i: (0, i))] * (len(xs) + len(cots))
        + [whole(b.shape) for b in (*backs, *hiddens)],
        [like((width, cols), BF)],
        [pl.BlockSpec((tile, cols), lambda i: (i, 0))],
        2 * len(xs) * half * width * cols,
        grid=(width // tile,),
    )[0]


def body(
    n_dp,
    n_ctx,
    tokens,
    cotangent,
    lengths,
    deal_order,
    routes,
    attn_gain,
    q_weight,
    kv_down,
    latent_gain,
    kv_up,
    out_weight,
    ffn_gain,
    router,
    shared_gate,
    shared_up,
    shared_down,
    expert_gate,
    expert_up,
    expert_down,
):
    rows, width = tokens.shape
    half = rows // 2
    top = routes.shape[1]
    experts = router.shape[1]
    blocks = n_dp * n_ctx
    band = width // blocks
    slots = 4 * rows * top // (3 * experts) // 2
    z = lax.axis_index("dp")
    c = lax.axis_index("ctx")
    t = lax.axis_index("tp")
    expert_id = z * n_ctx + c
    width_qk = NOPE + ROPE
    width_kv = NOPE + VDIM
    scale_factor = width_qk ** (-0.5)
    heads = q_weight.shape[1] // width_qk // n_ctx
    pack = rows * n_ctx

    def across(x, j):
        return lax.ppermute(x, "ctx", [(i, i ^ j) for i in range(n_ctx)])

    def swap(x):
        return lax.ppermute(x, "tp", [(0, 1), (1, 0)])

    def hop(x):
        return lax.ppermute(x, "dp", [(i, (i + 1) % n_dp) for i in range(n_dp)])

    def own_half(x):
        return lax.dynamic_slice_in_dim(x, t * half, half)

    def both_halves(x):
        other = swap(x)
        first = t == 0
        return jnp.concatenate([jnp.where(first, x, other), jnp.where(first, other, x)], axis=0)

    def gather_parts(x, *marks):
        near = [x] + after([across(x, j) for j in range(1, n_ctx)], *marks)
        return near + [swap(p) for p in near]

    def scatter_pack(near, far):
        near = (near + swap(far).astype(F32)).astype(BF)
        sent = near.reshape(n_ctx, half, near.shape[1])
        return lax.all_to_all(sent, "ctx", split_axis=0, concat_axis=0, tiled=True), sent

    def gathered(parts, *marks):
        return jnp.sum(after(parts, *marks).astype(F32), axis=0)

    def after(values, *marks):
        return lax.optimization_barrier((values, *marks))[0]

    q_cols, out_rows = heads * width_qk, heads * VDIM
    up_cols = heads * width_kv
    up_rows = kv_up.shape[0]
    folds = up_cols // LANES
    lead_cols = q_cols + LANES
    nope_cols = heads * NOPE

    def plane_order(near):
        bit = 1
        while bit < n_ctx:
            shape = near.shape
            pairs = near.reshape((n_ctx // (2 * bit), 2, bit) + shape[1:])
            near = jnp.where((c & bit) > 0, pairs[:, ::-1], pairs).reshape(shape)
            bit *= 2
        return near

    def ring_of(x):
        ring = [x]
        for _ in range(n_dp - 1):
            ring.append(hop(ring[-1]))
        return ring

    def collect(ring, take, block):
        total = None
        for k, x in enumerate(ring):
            part = take(x)
            if total is None:
                total = jnp.zeros((n_dp * block,) + part.shape[1:], part.dtype)
            total = lax.dynamic_update_slice_in_dim(total, part, ((z - k) % n_dp) * block, 0)
        return total

    small = jnp.concatenate([attn_gain, ffn_gain, latent_gain, router.reshape(band * experts)])
    small_rows = -(-small.shape[0] // lead_cols)
    small = jnp.pad(small, (0, small_rows * lead_cols - small.shape[0]))
    small = small.reshape(small_rows, lead_cols)

    def lead_piece(j):
        q = lax.dynamic_slice_in_dim(q_weight, (c ^ j) * q_cols, q_cols, 1)
        q = q.reshape(band, heads, width_qk)
        q = jnp.concatenate(
            [q[..., :NOPE].reshape(band, nope_cols), q[..., NOPE:].reshape(band, -1)], axis=1
        )
        up = lax.dynamic_slice_in_dim(kv_up, (c ^ j) * up_cols, up_cols, 1)
        up = up.reshape(up_rows, folds, LANES).transpose(1, 0, 2).reshape(folds * up_rows, LANES)
        return jnp.concatenate([jnp.concatenate([q, up], axis=1), small], axis=0)

    def out_piece(j):
        return lax.dynamic_slice_in_dim(out_weight, (c ^ j) * out_rows, out_rows, 0)

    lead = [lead_piece(0)] + [across(lead_piece(j), j) for j in range(1, n_ctx)]
    lead = plane_order(jnp.stack(lead))
    own_tokens_low = own_half(tokens)
    token_parts = gather_parts(after(own_tokens_low, lead))
    lead_ring = ring_of(lead)
    q_mine = collect(lead_ring, lambda x: x[:, :band, :q_cols].reshape(-1, q_cols), n_ctx * band)
    up_mine = collect(
        lead_ring,
        lambda x: x[:, :band, q_cols:]
        .reshape(n_ctx, folds, up_rows, LANES)
        .transpose(0, 2, 1, 3)
        .reshape(n_ctx * up_rows, up_cols),
        n_ctx * up_rows,
    )
    small_all = collect(lead_ring, lambda x: x[:, band:], n_ctx).reshape(blocks, -1)
    attn_gain_all = small_all[:, :band].reshape(width).astype(F32)
    ffn_gain_all = small_all[:, band : 2 * band].reshape(width).astype(F32)
    latent_cols = latent_gain.shape[0]
    latent_gain_all = (
        small_all[:, 2 * band : 2 * band + latent_cols].reshape(KV_RANK).astype(F32)
    )
    router_all = small_all[:, 2 * band + latent_cols : 2 * band + latent_cols + band * experts]
    router_all = router_all.reshape(width, experts)

    down_half = lax.dynamic_slice_in_dim(kv_down, t * (band // 2), band // 2)
    down_all = lax.all_gather(down_half, ("dp", "ctx", "tp"), axis=0, tiled=True)

    out_near = plane_order(
        jnp.stack([out_piece(0)] + [across(after(out_piece(j), q_mine), j) for j in range(1, n_ctx)])
    )
    out_mine = (
        lax.all_gather(out_near, "dp", axis=0, tiled=True)
        .transpose(1, 0, 2)
        .reshape(out_rows, width)
    )

    groups = -(-shared_gate.shape[1] // (LANES * n_dp))
    hidden_units = groups * LANES
    all_units = hidden_units * n_dp

    def widen(x, cols):
        return jnp.pad(x, ((0, 0), (0, cols - x.shape[1])))

    def unit_pieces(w):
        return widen(w, all_units).reshape(band, n_dp, hidden_units).transpose(1, 0, 2)

    units = expert_gate.shape[2]
    padded_units = -(-units // 256) * 256
    gate_w, up_w, expert_out = (
        after(jnp.pad(w, ((0, padded_units - units), (0, 0))), lead_ring[1])
        for w in (expert_gate[0].T, expert_up[0].T, expert_down[0])
    )

    plane = c.astype(jnp.int32).reshape(1)
    order_index = jnp.arange(n_ctx)[None, :] * 2 + (t ^ jnp.arange(2))[:, None]
    order_row = deal_order[0].reshape(n_ctx * 2, half)[order_index.reshape(-1)].reshape(pack)
    docs, pos = places(lengths[0], order_row)
    cos_table, sin_table = rope_tables(pos)
    own_cot = own_half(cotangent)
    expert_row = jnp.arange(experts, dtype=jnp.int32)
    hot = jnp.sum((routes[:, :, None] == expert_row[None, None, :]).astype(BF), axis=1)
    row_index = jnp.arange(rows)
    earlier = (row_index[:, None] >= row_index[None, :]).astype(BF)
    rank = dot(earlier, hot) * hot.astype(F32)

    cot_extended = jnp.concatenate(
        [own_cot, own_half(rank).astype(BF), jnp.zeros((half, LANES - experts), BF)], axis=1
    )
    ids = jnp.concatenate(
        [
            (z * n_ctx + jnp.arange(n_ctx, dtype=jnp.int32)).astype(jnp.int32),
            (t * slots + 1).astype(jnp.int32).reshape(1),
        ]
    )

    apart = n_ctx if slots % 16 == 0 else 1
    near_ids = ids
    if apart > 1:
        near_ids = jnp.concatenate(
            [(z * n_ctx + (c ^ jnp.arange(n_ctx, dtype=jnp.int32))).astype(jnp.int32), ids[n_ctx:]]
        )

    def exchange(x):
        total, cols = x.shape
        x = x.reshape(n_ctx, total // n_ctx, cols)
        x = lax.all_to_all(x, "ctx", split_axis=0, concat_axis=0, tiled=True)
        return x.reshape(total, cols)

    def send_slots(parts):
        if apart == 1:
            return [exchange(parts[0])]
        return [parts[0]] + [across(parts[j], j) for j in range(1, n_ctx)]

    def both_cores(parts):
        return parts + [swap(p) for p in parts]

    cot_pairs, cot_parts = [], []

    def cot_step(x):
        pair = (x, swap(x))
        picked = pick_rows(near_ids, slots, pair, pair, width, width, apart)
        cot_pairs.append(pair)
        cot_parts.append(send_slots(picked))

    cot_step(cot_extended)
    normed_low = norm_rows(plane, after(token_parts, cot_parts[0]), attn_gain_all)
    query_pre = dot(normed_low, q_mine)
    query_turned = rotate(
        query_pre[:, nope_cols:].reshape(pack, heads, ROPE),
        cos_table[:, None],
        sin_table[:, None],
    )
    latent_pre = dot(normed_low, down_all)
    latent_low = rmsnorm(latent_pre[:, :KV_RANK], latent_gain_all).astype(BF)
    rope_low = rotate(latent_pre[:, KV_RANK:], cos_table, sin_table).astype(BF)
    if n_dp > 1:
        cot_step(after(hop(after(cot_extended, q_mine)), latent_low))
    expanded = dot(latent_low, up_mine).astype(BF)
    allowed = (docs[:, None] == docs[None, :]) & (pos[None, :] <= pos[:, None])
    queries, keys, values, log_totals, attended = [], [], [], [], []

    def scores_of(h):
        return jnp.where(allowed, dot_nt(queries[h], keys[h]) * scale_factor, NEGATIVE)

    for h in range(heads):
        queries.append(
            jnp.concatenate(
                [query_pre[:, h * NOPE : (h + 1) * NOPE], query_turned[:, h]], axis=1
            ).astype(BF)
        )
        base = h * width_kv
        keys.append(jnp.concatenate([expanded[:, base : base + NOPE], rope_low], axis=1))
        values.append(expanded[:, base + NOPE : base + width_kv])
        scores = scores_of(h)
        highest = jnp.max(scores, axis=-1, keepdims=True)
        exponentials = jnp.exp(scores - highest)
        totals = jnp.sum(exponentials, axis=-1, keepdims=True)
        log_totals.append(highest + jnp.log(totals))
        attended.append(dot((exponentials / totals).astype(BF), values[h]).astype(BF))
    first_attended = attended[0]

    attended = jnp.concatenate(attended, axis=1)
    own_tokens = own_tokens_low.astype(F32)
    middle = pack // 2
    attended = after(attended, cot_parts[-1])
    attended_far = dot(attended[middle:], out_mine).astype(BF)
    attended_parts, attended_sent = scatter_pack(dot(attended[:middle], out_mine), attended_far)

    if n_dp > 2:
        cot_step(after(hop(cot_pairs[1][0]), attended_sent))
    order = list(range(1, n_dp)) + [0]
    groups = [tuple(order[i : i + 2]) for i in range(0, n_dp, 2)]

    def cot_pieces(group):
        if apart > 1:
            return [cot_parts[k][j] for j in range(n_ctx) for k in group]
        near = [cot_parts[k][0].reshape(n_ctx, slots, width) for k in group]
        return [jnp.stack(near, axis=1).reshape(-1, width)]

    hidden_one = own_tokens + gathered(attended_parts, gate_w, up_w)
    for k in range(3, n_dp):
        cot_step(after(hop(cot_pairs[k - 1][0]), attended_sent))

    ffn_normed, ffn_norm_back = jax.vjp(rmsnorm, hidden_one, ffn_gain_all)
    ffn_low = ffn_normed.astype(BF)
    router_probs = jax.nn.softmax(dot(ffn_low, router_all), axis=-1)
    probs_high, probs_low = two_parts(router_probs)
    spare = jnp.zeros((half, LANES - 2 * experts), BF)
    ffn_ring = ring_of(jnp.concatenate([ffn_low, probs_high, probs_low, spare], axis=1))
    shared_send = jnp.concatenate(
        [unit_pieces(w)
            for w in after((shared_gate, shared_up, shared_down.T), ffn_ring[min(2, n_dp - 1)])], axis=2
    )
    shared_part = lax.all_to_all(
        shared_send, "dp", split_axis=0, concat_axis=0, tiled=True
    )
    shared_all = (
        lax.all_gather(shared_part, "ctx", axis=0, tiled=False)
        .transpose(1, 0, 2, 3)
        .reshape(width, 3 * hidden_units)
    )
    shared_in = shared_all[:, : 2 * hidden_units]
    shared_out_t = shared_all[:, 2 * hidden_units :]
    first = jnp.stack([expert_id, c]).astype(jnp.int32)

    mark = [attended_sent]

    def in_turn(run, args, *rest):
        result = run(*after(args, mark[0]), *rest)
        mark[0] = result[0] if isinstance(result, (list, tuple)) else result
        return result

    products = {}
    pairs, x_near, x_in, shared_hidden, back_shared_pre = {}, {}, {}, {}, {}
    nears, fars, returned, combined = {}, {}, {}, {}
    x_rows, back_gates, back_ups, gated = [], [], [], []

    def product_chunk(group):
        products[group] = in_turn(
            lambda *near: cot_product(both_cores(list(near)), expert_out), cot_pieces(group)
        )

    def ranked_of(group):
        return [x for k in group for x in cot_pairs[k]]

    def pick_chunk(group):
        pairs[group] = [x for k in group for x in (ffn_ring[k], swap(ffn_ring[k]))]
        picked = in_turn(
            lambda *blocks: pick_rows(
                near_ids, slots, ranked_of(group), blocks, width, width + LANES, apart
            ),
            pairs[group],
        )
        x_near[group] = send_slots(picked)

    def share_chunk(group):
        back_shared_pre[group], shared_hidden[group] = in_turn(
            lambda *blocks: shared_chunk(blocks, shared_in, [back_shared[k] for k in group]),
            pairs[group],
        )

    def run_expert(group):
        x, back_gate, back_up, gated_hidden, *near, far = in_turn(
            lambda *parts: expert_chunk(
                list(parts), experts, first, products[group][0], gate_w, up_w, expert_out
            ),
            x_in[group],
        )
        x_rows.append(x)
        back_gates.append(back_gate)
        back_ups.append(back_up)
        gated.append(gated_hidden)
        nears[group] = near
        fars[group] = swap(far)

    def merge_chunk(group):
        merged = in_turn(
            lambda *parts: merge_rows(experts, apart, first, *parts),
            (*nears[group], fars[group]),
        )
        returned[group] = send_slots(merged)

    def combine_chunk(group):
        sums = in_turn(
            lambda *parts: combine_rows(
                near_ids,
                slots,
                ranked_of(group),
                parts,
                shared_hidden[group],
                shared_out_t,
                back_shared_pre[group],
                shared_in,
            ),
            returned[group],
        )
        combined.update(zip(group, sums))

    product_chunk(groups[0])
    pick_chunk(groups[0])
    for p, group in enumerate(groups):
        x_in[group] = both_cores(after(x_near[group], mark[0]))
        if p + 1 < len(groups):
            pick_chunk(groups[p + 1])
        run_expert(group)
        if p == 0:
            back_shared = in_turn(
                lambda *flat: cot_shared(
                    [flat[2 * i : 2 * i + 2] for i in range(n_dp)], shared_out_t
                ),
                [x for pair in cot_pairs for x in pair],
            )
            share_chunk(group)
        else:
            combine_chunk(groups[p - 1])
        merge_chunk(group)
        if p + 1 < len(groups):
            product_chunk(groups[p + 1])
            share_chunk(groups[p + 1])
    cot_rows = [products[group][1] for group in groups]
    shared_backs = [back_shared_pre[group] for group in groups]
    shared_hiddens = [shared_hidden[group] for group in groups]
    grad_egate, grad_eup = in_turn(
        lambda *gates: weight_grads([gates, back_ups], [x_rows], ((0, 2), (1, 2)), units),
        back_gates,
    )
    x_pairs = [x for group in groups for x in pairs[group]]
    cot_flat = [x for group in groups for x in ranked_of(group)]
    totals = []

    def add_chunk(k):
        near, far = combined[k]
        near = near + swap(far).astype(F32)
        if totals:
            moved = hop(totals[-1].astype(BF))
            near = near + (after(moved, grad_egate) if k in order[:-2] else moved).astype(F32)
        totals.append(near)

    for k in order[:-2]:
        add_chunk(k)
    if totals:
        mark[0] = (mark[0], totals[-1])
    grad_shared = in_turn(
        lambda *xs: shared_grads(xs, cot_flat, shared_backs, shared_hiddens, width), x_pairs
    )
    grad_shared = grad_shared.reshape(n_dp, n_ctx, band, 3 * hidden_units)
    grad_shared = grad_shared.transpose(1, 0, 2, 3).reshape(width, 3 * hidden_units)
    mark[0] = grad_shared
    combine_chunk(groups[-1])
    for k in order[-2:]:
        add_chunk(k)
    total = totals[-1]
    output_sum, back_ffn = total[:, :width], total[:, width:]
    back_probs = (
        back_ffn[:, width : width + experts] + back_ffn[:, width + experts : width + 2 * experts]
    )
    back_logits = router_probs * (
        back_probs - jnp.sum(router_probs * back_probs, axis=-1, keepdims=True)
    )
    back_ffn_normed = back_ffn[:, :width] + jnp.dot(
        back_logits, router_all.astype(F32).T, precision=PRECISE
    )
    grad_router = jnp.dot(back_logits.T, ffn_low.astype(F32), precision=PRECISE)
    back_hidden_one, grad_ffn_gain = ffn_norm_back(back_ffn_normed)
    back_hidden_one = back_hidden_one + own_cot.astype(F32)

    mark[0] = back_hidden_one
    (grad_edown,) = in_turn(
        lambda *gates: weight_grads([gates], [cot_rows], ((0, 1),), units), gated
    )
    back_parts = gather_parts(back_hidden_one.astype(BF), grad_edown)
    output = both_halves((hidden_one + output_sum).astype(BF))

    back_attended, grad_out_t = attended_back(plane, back_parts, out_mine, attended)
    grad_shared = lax.psum_scatter(
        after(grad_shared, back_parts), "ctx", scatter_dimension=0, tiled=True
    )
    grad_out_t = lax.psum_scatter(grad_out_t, "dp", scatter_dimension=1, tiled=True)
    back_nope, back_turned, back_expanded, back_rope = [], [], [], None
    for h in range(heads):
        back_head = back_attended[:, h * VDIM : (h + 1) * VDIM]
        probabilities = jnp.exp(scores_of(h) - log_totals[h])
        back_prob = dot_nt(back_head, values[h])
        inner_sum = jnp.sum(probabilities * back_prob, axis=-1, keepdims=True)
        back_raw = (probabilities * (back_prob - inner_sum) * scale_factor).astype(BF)
        back_query = dot(back_raw, keys[h])
        back_key = dot_tn(back_raw, queries[h])
        back_nope.append(back_query[:, :NOPE].astype(BF))
        back_turned.append(unrotate(back_query[:, NOPE:], cos_table, sin_table).astype(BF))
        back_expanded.append(back_key[:, :NOPE].astype(BF))
        back_expanded.append(dot_tn(probabilities.astype(BF), back_head).astype(BF))
        turned = back_key[:, NOPE:]
        back_rope = turned if back_rope is None else back_rope + turned
    grad_shared_sum = grad_shared
    grad_shared = grad_shared.reshape(n_dp, band, 3 * hidden_units)
    shared_near = [lax.dynamic_index_in_dim(grad_shared, z, 0, keepdims=False)]
    for i in range(1, n_dp):
        sent = lax.dynamic_index_in_dim(grad_shared, (z + i) % n_dp, 0, keepdims=False)
        shared_near.append(
            lax.ppermute(sent, "dp", [(a, (a + i) % n_dp) for a in range(n_dp)])
        )
    grad_shared = shared_near
    back_nope = after(back_nope, grad_shared_sum)
    back_query_pre = jnp.concatenate(back_nope + back_turned, axis=1)
    back_expanded = jnp.concatenate(back_expanded, axis=1)
    back_latent = jnp.concatenate(
        [dot_nt(back_expanded, up_mine), back_rope, jnp.zeros((pack, ROPE), F32)], axis=1
    )
    latent_near = back_latent[:middle] + swap(back_latent[middle:].astype(BF)).astype(F32)
    latent_near = latent_near.astype(BF).reshape(n_ctx, half, -1)
    latent_parts = jnp.stack(
        [lax.dynamic_index_in_dim(latent_near, c, 0, keepdims=False)]
        + [
            across(lax.dynamic_index_in_dim(latent_near, c ^ j, 0, keepdims=False), j)
            for j in range(1, n_ctx)
        ]
    )
    grad_heads = jnp.concatenate(
        [
            dot_tn(normed_low, back_query_pre),
            dot_tn(latent_low, back_expanded)
            .reshape(blocks, up_rows, folds, LANES)
            .transpose(0, 2, 1, 3)
            .reshape(width, LANES),
        ],
        axis=1,
    ).astype(BF)
    back_query_pre = after(back_query_pre, grad_heads)
    back_far = dot_nt(back_query_pre[middle:], q_mine).astype(BF)
    back_near = dot_nt(back_query_pre[:middle], q_mine) + swap(back_far).astype(F32)
    back_near = back_near.astype(BF).reshape(n_ctx, half, width)
    back_sent = [
        lax.dynamic_index_in_dim(back_near, c ^ j, 0, keepdims=False) for j in range(n_ctx)
    ]
    back_sum_parts = [back_sent[0]] + [across(back_sent[j], j) for j in range(1, n_ctx)]
    back_latent = gathered(latent_parts, back_sent)
    own_rows = functools.partial(lax.dynamic_slice_in_dim, start_index=c * half, slice_size=half)
    own_latent = own_rows(latent_pre)[:, :KV_RANK]
    back_latent_pre, grad_latent_gain = jax.vjp(rmsnorm, own_latent, latent_gain_all)[1](
        back_latent[:, :KV_RANK]
    )
    back_down = jnp.concatenate(
        [
            back_latent_pre,
            unrotate(
                back_latent[:, KV_RANK : KV_RANK + ROPE], own_rows(cos_table), own_rows(sin_table)
            ),
        ],
        axis=1,
    ).astype(BF)
    back_near = plane_order(
        jnp.stack([back_down] + [across(back_down, j) for j in range(1, n_ctx)])
    )
    back_near = back_near.reshape(middle, back_down.shape[1])
    back_down_parts = [back_near, swap(back_near)]
    back_sum = sum(x.astype(F32) for x in back_sum_parts)
    back_normed = back_sum + dot_nt(back_down, down_all)
    back_inputs, grad_attn_gain = jax.vjp(rmsnorm, own_tokens, attn_gain_all)[1](back_normed)
    input_grad = both_halves(back_hidden_one + back_inputs)

    placed_shared = jnp.zeros((n_dp, band, 3 * hidden_units), F32)
    for i, part in enumerate(after(grad_shared, back_sent)):
        placed_shared = lax.dynamic_update_index_in_dim(
            placed_shared, part.astype(F32), (z - i) % n_dp, 0
        )
    grad_sgate, grad_sup, grad_sdown = (
        placed_shared[:, :, i * hidden_units : (i + 1) * hidden_units]
        .transpose(1, 0, 2)
        .reshape(band, all_units)[:, : shared_gate.shape[1]]
        for i in range(3)
    )

    grad_heads = lax.psum_scatter(grad_heads, "dp", scatter_dimension=0, tiled=True)
    grad_heads = lax.all_to_all(
        after(grad_heads, back_sum_parts).reshape(n_ctx, band, -1), "ctx", split_axis=0, concat_axis=0, tiled=True
    ).astype(F32)
    grad_q = jnp.concatenate(
        [
            grad_heads[:, :, :nope_cols].reshape(n_ctx, band, heads, NOPE),
            grad_heads[:, :, nope_cols:q_cols].reshape(n_ctx, band, heads, ROPE),
        ],
        axis=3,
    )
    grad_q = grad_q.transpose(1, 0, 2, 3).reshape(band, n_ctx * q_cols)
    grad_out = lax.all_to_all(
        after(grad_out_t, back_sum).reshape(out_rows, n_ctx, band).transpose(1, 0, 2),
        "ctx",
        split_axis=0,
        concat_axis=0,
        tiled=True,
    )
    grad_out = grad_out.astype(F32).reshape(n_ctx * out_rows, band)
    grad_up = (
        grad_heads[:, :, q_cols:]
        .reshape(n_ctx, folds, up_rows, LANES)
        .transpose(2, 0, 1, 3)
        .reshape(up_rows, n_ctx * up_cols)
    )
    back_down_pack = jnp.concatenate(back_down_parts, axis=0)
    normed_band = jnp.concatenate(
        [
            lax.dynamic_slice_in_dim(normed_low, (i * n_ctx + c) * band, band, axis=1)
            for i in range(n_dp)
        ],
        axis=1,
    )
    down_sums = dot_tn(normed_band, back_down_pack).reshape(n_dp, band, -1)
    grad_down = lax.dynamic_index_in_dim(down_sums, z, 0, keepdims=False)
    for i in range(1, n_dp):
        sent = lax.dynamic_index_in_dim(down_sums, (z + i) % n_dp, 0, keepdims=False)
        sent = lax.ppermute(sent.astype(BF), "dp", [(a, (a + i) % n_dp) for a in range(n_dp)])
        grad_down = grad_down + sent.astype(F32)
    late = jnp.concatenate(
        [
            grad_router.reshape(experts, blocks, band).transpose(1, 0, 2),
            grad_ffn_gain.reshape(blocks, 1, band),
            grad_attn_gain.reshape(blocks, 1, band),
            widen(grad_latent_gain.reshape(blocks, latent_cols), band)[:, None],
        ],
        axis=1,
    )
    late = jnp.sum(
        lax.all_to_all(late + swap(late), GRID, split_axis=0, concat_axis=0, tiled=True), axis=0
    )
    return (
        output,
        input_grad,
        late[experts + 1],
        grad_q,
        grad_down,
        late[experts + 2, :latent_cols],
        grad_up,
        grad_out,
        late[experts],
        late[:experts].T,
        grad_sgate,
        grad_sup,
        grad_sdown.T,
        grad_egate.T[None],
        grad_eup.T[None],
        grad_edown[None],
    )


def solution(mesh):
    n_dp, n_ctx = mesh.shape["dp"], mesh.shape["ctx"]
    ins = (
        P(GRID, None),
        P(GRID, None),
        P("dp", None),
        P("dp", None),
        P(GRID, None),
        P(GRID),
        P(GRID, "tp"),
        P(GRID, None),
        P(GRID),
        P(GRID, "tp"),
        P("tp", GRID),
        P(GRID),
        P(GRID, None),
        P(GRID, "tp"),
        P(GRID, "tp"),
        P("tp", GRID),
        P(GRID, None, "tp"),
        P(GRID, None, "tp"),
        P(GRID, "tp", None),
    )
    outs = (
        P(GRID, None),
        P(GRID, None),
        P(GRID),
        P(GRID, "tp"),
        P(GRID, None),
        P(GRID),
        P(GRID, "tp"),
        P("tp", GRID),
        P(GRID),
        P(GRID, None),
        P(GRID, "tp"),
        P(GRID, "tp"),
        P("tp", GRID),
        P(GRID, None, "tp"),
        P(GRID, None, "tp"),
        P(GRID, "tp", None),
    )
    return jax.shard_map(
        functools.partial(body, n_dp, n_ctx),
        mesh=mesh,
        in_specs=ins,
        out_specs=outs,
        check_vma=False,
    )
```
